32 devices in a mesh: gx: 2 (over x), yz: 16 (over z, y, core).
Axes of the slice: x: 2, y: 2, z: 4, core: 2. Of those that a mesh axis runs over, the one named last changes fastest.
Arguments:
- displacement: float32 [3, 8, 16, 8, 256], P(None, 'gx', 'yz'), may hold values from -0.04 to 0.04
- velocity: float32 [3, 8, 16, 8, 256], P(None, 'gx', 'yz'), may hold values from -5 to 5
- rest_length: float32 [18, 8, 16, 8, 256], P(None, 'gx', 'yz'), may hold values from 0.96 to 1.48, as said below
- heights: int32 [8, 32], replicated, may hold values from 512 to 1024
Outputs:
- new_displacement: float32 [3, 8, 16, 8, 256], P(None, 'gx', 'yz')
- half_velocity: float32 [3, 8, 16, 8, 256], P(None, 'gx', 'yz')
- boost_factor: float32 [], replicated
The draws below stay inside these ranges and needn't reach their ends.
Inputs may be any that keep to these rules, and one draw needn't show every extreme that they name: rest_length[k + 9] of an atom equals rest_length[k] of the atom -d_k away from it, wherever both atoms lie within the layers.
All inputs are finite; a program needn't handle non-finite values.
Results may differ from the reference program's by a relative error of at most 0.0003.
Values sent between devices are 32-bit elements; how exact they have to be, the bound alone decides.
A program may use at most 128 MiB of HBM per device.

```python
import jax
import jax.numpy as jnp
from jax import lax

CY = 8
CZ = 256
ZT = 4
YT = 4
TILES = 16
NX = 8
NY = 32
Z = 1024


def forward_bonds():
    chosen = []
    for along_x in (-1, 0, 1):
        for along_y in (-1, 0, 1):
            for along_z in (-1, 0, 1):
                length_sq = along_x * along_x + along_y * along_y + along_z * along_z
                if 0 < length_sq <= 2 and (along_x, along_y, along_z) > (0, 0, 0):
                    chosen.append((along_x, along_y, along_z))
    return chosen


def draw_rest_length(key, part):
    forward = forward_bonds()
    lengths = jnp.sqrt(jnp.array([float(vector[0] * vector[0] + vector[1] * vector[1] + vector[2] * vector[2]) for vector in forward], jnp.float32))
    spread = 0.04 * jnp.tanh(jax.random.normal(jax.random.fold_in(key, 21), (9, NX, NY, Z), jnp.float32))
    ahead = lengths[:, None, None, None] * (1.0 + spread)
    behind = [jnp.roll(ahead[position], (forward[position][0], forward[position][1], forward[position][2]), axis=(0, 1, 2)) for position in range(9)]
    lattice = jnp.concatenate([ahead, jnp.stack(behind)], axis=0).astype(jnp.float32)
    blocks = lattice.reshape(18, NX, YT, CY, ZT, CZ)
    ordered = jnp.transpose(blocks, (0, 1, 2, 4, 3, 5)).reshape(18, NX, YT * ZT, CY, CZ)
    return jnp.roll(ordered, -(ZT // 2), axis=2)


def draw_heights(key, part):
    values = jax.random.randint(jax.random.fold_in(key, 31), (NX * NY,), Z // 2, Z + 1)
    spots = jax.random.permutation(jax.random.fold_in(key, 32), NX * NY)
    values = values.at[spots[0]].set(Z).at[spots[1]].set(Z // 2)
    return values.reshape(NX, NY).astype(jnp.int32)


def levels(rng, dims, split, smallest, top_value):
    def one(axis_at, blocks):
        steps = jax.random.uniform(jax.random.fold_in(jax.random.fold_in(rng, 6), axis_at), (blocks,), jnp.float32, smallest / len(split), top_value / len(split))
        return jnp.repeat(jnp.exp(steps), dims[axis_at] // blocks).reshape((-1,) + (1,) * (len(dims) - axis_at - 1))

    factor_of = one(*split[0])
    for cut in split[1:]:
        factor_of = factor_of * one(*cut)
    return factor_of


def gaussian(own_key, shape, scale, limit, shards=(), dtype=jnp.bfloat16):
    level = levels(own_key, shape, shards, -0.22, 0.18) if shards else 1.0
    entries = jax.random.normal(own_key, shape, jnp.float32) * scale * level
    return jnp.minimum(jnp.maximum(entries, -limit), limit).astype(dtype)


def setup_inputs(seed: int = 0) -> dict:
    key_of = jax.random.split(jax.random.key(seed), 5)
    displacement = gaussian(key_of[0], (3, NX, TILES, CY, CZ), 0.016, 0.04, ((1, 2), (2, 16)), jnp.float32)
    velocity = gaussian(key_of[1], (3, NX, TILES, CY, CZ), 1.0, 5.0, ((1, 2), (2, 16)), jnp.float32)
    rest_length = draw_rest_length(jax.random.fold_in(key_of[4], 71), 0)
    heights = draw_heights(jax.random.fold_in(key_of[4], 71), 0)
    return dict(displacement=displacement, velocity=velocity, rest_length=rest_length, heights=heights)


CUTOFF = 1.5
REACH_RADIUS = 3.5
DENSITY_DECAY = 3.0
PAIR_DECAY = 6.0
PAIR_SCALE = 0.6
EMBED_SCALE = 1.0
DENSITY_FLOOR = 0.5
SHARPNESS = 8.0
STRAIN_LIMIT = 0.1
BIAS_SCALE = 0.08
KICK_FACTOR = 0.2
TIME_STEP = 0.05
THERMAL = 0.5

def list_offsets(reach_sq, forward_only):
    chosen = []
    for along_x in range(-3, 4):
        for along_y in range(-3, 4):
            for along_z in range(-3, 4):
                length_sq = along_x * along_x + along_y * along_y + along_z * along_z
                if 0 < length_sq <= reach_sq:
                    if not forward_only or (along_x, along_y, along_z) > (0, 0, 0):
                        chosen.append((along_x, along_y, along_z))
    return chosen

def bond_offsets():
    forward = list_offsets(2, True)
    return forward + [(-vector[0], -vector[1], -vector[2]) for vector in forward]

def taper_value(radius, cutoff):
    inside = 1.0 - (radius / cutoff) ** 2
    return jnp.where(radius < cutoff, inside * inside, 0.0)

def taper_slope(radius, cutoff):
    inside = 1.0 - (radius / cutoff) ** 2
    return jnp.where(radius < cutoff, -4.0 * radius * inside / (cutoff * cutoff), 0.0)

def to_lattice(tiled):
    channels, row_count = (tiled.shape[0], tiled.shape[1])
    ordered = jnp.roll(tiled, ZT // 2, axis=2)
    blocks = ordered.reshape(channels, row_count, YT, ZT, CY, CZ)
    return jnp.transpose(blocks, (0, 1, 2, 4, 3, 5)).reshape(channels, row_count, YT * CY, ZT * CZ)

def to_tiles(lattice):
    channels, row_count = (lattice.shape[0], lattice.shape[1])
    blocks = lattice.reshape(channels, row_count, YT, CY, ZT, CZ)
    ordered = jnp.transpose(blocks, (0, 1, 2, 4, 3, 5)).reshape(channels, row_count, YT * ZT, CY, CZ)
    return jnp.roll(ordered, -(ZT // 2), axis=2)

def shifted(source, offset):
    rolled = jnp.roll(source, (-offset[0], -offset[1]), axis=(-3, -2))
    padded = jnp.pad(rolled, [(0, 0)] * (source.ndim - 1) + [(3, 3)])
    layers = source.shape[-1]
    return padded[..., 3 + offset[2]:3 + offset[2] + layers]

def separation(displacement, offset):
    beside = shifted(displacement, offset)
    pieces = [offset[component] + beside[component] - displacement[component] for component in range(3)]
    radius = jnp.sqrt(pieces[0] * pieces[0] + pieces[1] * pieces[1] + pieces[2] * pieces[2])
    return (pieces, radius)

def reference(displacement, velocity, rest_length, heights):
    displacement = to_lattice(displacement)
    velocity = to_lattice(velocity)
    rest_length = to_lattice(rest_length)
    layers = displacement.shape[-1]
    layer_index = lax.broadcasted_iota(jnp.int32, (heights.shape[0], heights.shape[1], layers), 2)
    present = (layer_index < heights[:, :, None]).astype(jnp.float32)
    bond_list = bond_offsets()
    reach_list = list_offsets(9, False)
    density = jnp.zeros(present.shape, jnp.float32)
    bond_energy = jnp.zeros(present.shape, jnp.float32)
    bond_room = jnp.zeros(present.shape, jnp.float32)
    for bond_index in range(18):
        offset = bond_list[bond_index]
        pieces, radius = separation(displacement, offset)
        partner = shifted(present, offset)
        paired = present * partner
        density = density + partner * jnp.exp(-DENSITY_DECAY * (radius - 1.0)) * taper_value(radius, CUTOFF)
        relative = (radius - rest_length[bond_index]) / (rest_length[bond_index] * STRAIN_LIMIT)
        squared = relative * relative
        bond_energy = bond_energy + paired * jnp.exp(SHARPNESS * squared)
        bond_room = bond_room + paired * (1.0 - squared)
    embed_slope = -0.5 * EMBED_SCALE / jnp.sqrt(density + DENSITY_FLOOR)
    smooth_total = 1.0 + bond_energy
    for offset in reach_list:
        pieces, radius = separation(displacement, offset)
        smooth_total = smooth_total + taper_value(radius, REACH_RADIUS) * shifted(bond_energy, offset)
    smooth_max = jnp.log(smooth_total) / SHARPNESS
    bias_gain = BIAS_SCALE / (1.0 + smooth_max * smooth_max)
    bias_energy = present * bias_gain * bond_room
    adjoint_total = present * bond_room * BIAS_SCALE * (-2.0 * smooth_max) / (1.0 + smooth_max * smooth_max) ** 2 / (SHARPNESS * smooth_total)
    forces = [jnp.zeros(present.shape, jnp.float32) for component in range(3)]
    adjoint_lambda = adjoint_total
    for offset in reach_list:
        pieces, radius = separation(displacement, offset)
        far_adjoint = shifted(adjoint_total, offset)
        far_energy = shifted(bond_energy, offset)
        weight = (adjoint_total * far_energy + far_adjoint * bond_energy) * taper_slope(radius, REACH_RADIUS) / radius
        forces = [forces[component] + weight * pieces[component] for component in range(3)]
        adjoint_lambda = adjoint_lambda + taper_value(radius, REACH_RADIUS) * far_adjoint
    for bond_index in range(18):
        offset = bond_list[bond_index]
        pieces, radius = separation(displacement, offset)
        paired = present * shifted(present, offset)
        cut_value = taper_value(radius, CUTOFF)
        cut_slope = taper_slope(radius, CUTOFF)
        density_slope = jnp.exp(-DENSITY_DECAY * (radius - 1.0)) * (cut_slope - DENSITY_DECAY * cut_value)
        pair_slope = PAIR_SCALE * jnp.exp(-PAIR_DECAY * (radius - 1.0)) * (cut_slope - PAIR_DECAY * cut_value)
        relative = (radius - rest_length[bond_index]) / (rest_length[bond_index] * STRAIN_LIMIT)
        squared = relative * relative
        lifted = jnp.exp(SHARPNESS * squared)
        strain_slope = 2.0 * relative / (rest_length[bond_index] * STRAIN_LIMIT)
        far_slope = shifted(embed_slope, offset)
        far_gain = shifted(bias_gain, offset)
        far_lambda = shifted(adjoint_lambda, offset)
        coupled = paired * (pair_slope + (embed_slope + far_slope) * density_slope + (SHARPNESS * (adjoint_lambda + far_lambda) * lifted - bias_gain - far_gain) * strain_slope)
        weight = coupled / radius
        forces = [forces[component] + weight * pieces[component] for component in range(3)]
    half_velocity = velocity + KICK_FACTOR * jnp.stack(forces)
    new_displacement = displacement + TIME_STEP * half_velocity
    boost_factor = jnp.sum(present * jnp.exp(bias_energy / THERMAL)) / jnp.sum(present)
    return (to_tiles(new_displacement), to_tiles(half_velocity), boost_factor)
```

```python
import functools

import jax
import jax.numpy as jnp
from jax import lax
from jax.experimental import pallas as pl
from jax.experimental.pallas import tpu as pltpu
from jax.sharding import PartitionSpec as P

CUTOFF_SQ = 1.5 * 1.5
REACH_SQ = 3.5 * 3.5
F32 = jnp.float32
MESH = pl.DeviceIdType.MESH


def list_offsets(reach_sq, forward_only):
    chosen = []
    for ax in range(-3, 4):
        for ay in range(-3, 4):
            for az in range(-3, 4):
                length_sq = ax * ax + ay * ay + az * az
                if 0 < length_sq <= reach_sq:
                    if not forward_only or (ax, ay, az) > (0, 0, 0):
                        chosen.append((ax, ay, az))
    return chosen


FORWARD = list_offsets(2, True)
BONDS = FORWARD + [(-v[0], -v[1], -v[2]) for v in FORWARD]
REACH = list_offsets(9, False)
SHIFTS = [(dx, dz) for dx in range(-3, 4) for dz in range(-3, 4) if dx * dx + dz * dz <= 9]
SHIFTS_NEAR = [(dx, dz) for dx in range(-1, 2) for dz in range(-1, 2)]

NEAR, FAR, ENERGY, ADJOINT, SLOPES, LAMBDA = range(6)
ROUNDS = [(3, 1, 1), (3, 2, 3), (1, 1, 3), (1, 1, 3), (2, 1, 1), (1, 1, 1)]
Q_ENERGY, Q_ADJOINT, Q_LAMBDA, Q_EMBED, Q_GAIN = range(3, 8)
LEAD = 4
BAND = 16


def kernel(n_gx, n_yz, z_tiles, heights_hbm, disp, rest_hbm, forces, boost, *scratch):
    (x_disp, x_energy, x_adjoint, x_slopes, x_lambda) = scratch[0:5]
    ys = scratch[5:11]
    yr = scratch[11:17]
    scratch = scratch[3:]
    (z_mid, z_edge_out, z_edge, rest_out, rest_in) = scratch[14:19]
    (plain, edges, store, strip, strip_own, hb, hs, squares, pulls, bonds, part, first, sums) = scratch[19:32]
    (gains, rest_strip, rest, heights) = scratch[32:36]
    (send_sem, recv_sem, red_send, red_recv, load_sem) = scratch[36:41]
    x_of = [x_disp, x_disp, x_energy, x_adjoint, x_slopes, x_lambda]
    nx_all, ny_all = heights.shape
    loads = [
        pltpu.make_async_copy(heights_hbm, heights, load_sem.at[0]),
        pltpu.make_async_copy(rest_hbm, rest, load_sem.at[1]),
    ]
    planes, rows, cols = disp.shape[1], disp.shape[3], disp.shape[4]
    for half in range(2):
        for p in range(planes):
            loads.append(
                pltpu.make_async_copy(
                    disp.at[:, p, 0, :, half * 128 : half * 128 + 128],
                    x_disp.at[0, :, 2 * p + half],
                    load_sem.at[2 + 2 * p + half],
                )
            )
    for load in loads[2:] + loads[:2]:
        load.start()
    n_tiles = 2 * planes
    width = 128 // planes
    ext = width // 4
    y_tiles = n_yz // z_tiles
    gx = lax.axis_index("gx")
    me = lax.axis_index("yz")
    h = me + z_tiles // 2
    y_tile = lax.rem(h // z_tiles, y_tiles)
    z_tile = lax.rem(h, z_tiles)
    x_steps = [0, 1] if n_gx == 2 else [0, 1, -1]
    n_slots = len(x_steps)
    steps = [0, 1, -1]
    left_slot, right_slot = 1, n_slots - 1

    targets = {}

    def target(a, b, c):
        if (a, b, c) not in targets:
            to_y = lax.rem(y_tile + b + y_tiles, y_tiles)
            to_z = lax.rem(z_tile + c + z_tiles, z_tiles)
            to = lax.rem(to_y * z_tiles + to_z + n_yz - z_tiles // 2, n_yz)
            targets[(a, b, c)] = (lax.rem(gx + a + n_gx, n_gx), to)
        return targets[(a, b, c)]

    n_dev = n_gx * n_yz
    rank = gx * n_yz + me
    barrier = pltpu.get_barrier_semaphore()

    def greet(k, carry):
        to = lax.rem(rank + k, n_dev)
        pl.semaphore_signal(barrier, inc=1, device_id=(to // n_yz, lax.rem(to, n_yz)), device_id_type=MESH)
        return carry

    lax.fori_loop(1, n_dev, greet, 0)

    lane = lax.broadcasted_iota(jnp.int32, (8, 128), 1)
    spot = lax.rem(lane, width)

    def x_messages(r):
        buf = x_of[r]
        top = n_tiles - 2
        if r in (NEAR, SLOPES, LAMBDA):
            out = [
                (buf.at[0, :, top : n_tiles + 1], buf.at[left_slot, :, top : n_tiles + 1], 1),
                (buf.at[0, :, 0:2], buf.at[right_slot, :, 0:2], -1),
            ]
            if n_slots == 3:
                out.append((buf.at[0, :, n_tiles], buf.at[right_slot, :, n_tiles], -1))
        elif r == FAR:
            if n_slots == 2:
                out = [(buf.at[0, :, 2:top], buf.at[1, :, 2:top], 1)]
            else:
                out = [
                    (buf.at[0, :, 0:top], buf.at[left_slot, :, 0:top], 1),
                    (buf.at[0, :, 2:n_tiles], buf.at[right_slot, :, 2:n_tiles], -1),
                ]
        else:
            out = [(buf.at[0], buf.at[ai], x_steps[ai]) for ai in range(1, n_slots)]
        return [(src, dst, a, 0, 0) for src, dst, a in out]

    def messages(r):
        out = []
        if r == NEAR:
            for ai, a in reversed(list(enumerate(x_steps))):
                for ci in range(2):
                    for bi in range(2):
                        out.append((z_edge_out.at[bi], z_edge.at[ci, bi, ai], a, steps[1 + bi], steps[1 + ci]))
                    out.append((x_disp.at[0, :, n_tiles], z_mid.at[ci, ai], a, 0, steps[1 + ci]))
        far = []
        for ai, a in reversed(list(enumerate(x_steps))):
            for bi in range(2):
                far.append((ys[r].at[bi], yr[r].at[bi, ai], a, steps[1 + bi], 0))
        out = far + x_messages(r) + out
        if r == NEAR:
            for ci in range(2):
                out.append((rest_out, rest_in.at[ci], 0, 0, steps[1 + ci]))
        return [
            pltpu.make_async_remote_copy(
                src_ref=src,
                dst_ref=dst,
                send_sem=send_sem.at[r, i],
                recv_sem=recv_sem.at[r, i],
                device_id=target(a, b, c),
                device_id_type=MESH,
            )
            for i, (src, dst, a, b, c) in enumerate(out)
        ]

    copies = [messages(r) for r in range(len(ROUNDS))]

    def pack(r):
        count, low, high = ROUNDS[r]
        n_rows = high - low + 1
        for q in range(count):
            for t in range(n_tiles + 1):
                at = (q * (n_tiles + 1) + t) * n_rows
                ys[r][0, at : at + n_rows] = x_of[r][0, q, t, rows - high : rows - low + 1]
                ys[r][1, at : at + n_rows] = x_of[r][0, q, t, low - 1 : high]

    def send(r):
        for copy in copies[r]:
            copy.start()

    def receive(r):
        for copy in copies[r]:
            copy.wait_recv()

    def place_of(xp):
        if xp < 0:
            return left_slot, xp + planes
        if xp < planes:
            return 0, xp
        return right_slot, xp - planes

    def ghosts(r, q, t, slot):
        count, low, high = ROUNDS[r]
        n_rows = high - low + 1
        at = (q * (n_tiles + 1) + t) * n_rows
        return [
            (LEAD - high, LEAD - low + 1, yr[r][0, slot, at : at + n_rows]),
            (LEAD + rows + low - 1, LEAD + rows + high, yr[r][1, slot, at : at + n_rows]),
        ]

    def place(r, base, reach):
        for q in range(ROUNDS[r][0]):
            for xp in range(-reach, planes + reach):
                slot, plane = place_of(xp)
                at = xp + LEAD
                for half in range(2):
                    t = 2 * plane + half
                    if slot:
                        plain[base + q, half, at, LEAD : LEAD + rows] = x_of[r][slot, q, t]
                    for lo, hi, value in ghosts(r, q, t, slot) + (ghosts(NEAR, q, t, slot) if r == FAR else []):
                        plain[base + q, half, at, lo:hi] = value
            for slot in range(n_slots):
                if r != NEAR and r != FAR:
                    strip[base + q, slot, LEAD : LEAD + rows] = x_of[r][slot, q, n_tiles]
                    for lo, hi, value in ghosts(r, q, n_tiles, slot):
                        strip[base + q, slot, lo:hi] = value

    def blend(below, own, above):
        return jnp.where(spot < ext, below, jnp.where(spot >= width - ext, above, own))

    def strips_of_displacement(r):
        lane4 = lane[0:4]
        for q in range(3):
            for slot in range(n_slots):
                if r == NEAR:
                    strip[q, slot, LEAD : LEAD + rows] = blend(z_mid[0, slot, q], x_disp[slot, q, n_tiles], z_mid[1, slot, q])
                for bi, (lo, hi, value) in enumerate(ghosts(r, q, n_tiles, slot)):
                    first_row = lo - (0 if bi == 0 else LEAD + rows)
                    span = slice(first_row, first_row + hi - lo)
                    n = hi - lo
                    spot_n = spot[0:n]
                    strip[q, slot, lo:hi] = jnp.where(
                        spot_n < ext,
                        z_edge[0, bi, slot, q, span],
                        jnp.where(spot_n >= width - ext, z_edge[1, bi, slot, q, span], value),
                    )

    def shift_main(fields, reach, depth):
        inner = min(reach, max(1, reach - 1))
        spans = []
        for q in fields:
            for xp in range(-inner, planes + inner):
                for band in range(2):
                    spans.append((q, xp, band, slice(8 * band, 8 * band + 8)))
        for q, xp, band, span in spans:
            slot, plane = place_of(xp)
            edge = strip[q, slot, span]
            edges[q, 0, xp + LEAD, span] = pltpu.roll(edge, (128 - ext - width * plane) % 128, 1)
            edges[q, 1, xp + LEAD, span] = pltpu.roll(edge, (ext - width * plane - width) % 128, 1)
        for q, xp, band, span in spans:
            at = xp + LEAD
            t1 = plain[q, 0, at, span]
            t2 = plain[q, 1, at, span]
            low = edges[q, 0, at, span]
            high = edges[q, 1, at, span]
            for dz in range(1, depth + 1):
                if dz == 3 and not 3 - reach <= xp < planes + reach - 3:
                    continue
                up = lane < dz
                down = lane >= 128 - dz
                store[q, 3 + dz, 0, at, span] = pltpu.roll(jnp.where(up, t2, t1), 128 - dz, 1)
                store[q, 3 + dz, 1, at, span] = pltpu.roll(jnp.where(up, high, t2), 128 - dz, 1)
                store[q, 3 - dz, 0, at, span] = pltpu.roll(jnp.where(down, low, t1), dz, 1)
                store[q, 3 - dz, 1, at, span] = pltpu.roll(jnp.where(down, t1, t2), dz, 1)

    def shift_own(q, shifts):
        for band in range(2):
            span = slice(8 * band, 8 * band + 8)
            own, left, right = strip[q, 0, span], strip[q, left_slot, span], strip[q, right_slot, span]
            for dx, dz in shifts:
                s = width * dx + dz
                if s > 0:
                    value = pltpu.roll(jnp.where(lane >= s, own, right), 128 - s, 1)
                elif s < 0:
                    value = pltpu.roll(jnp.where(lane < 128 + s, own, left), -s, 1)
                else:
                    value = own
                strip_own[q, dx + 3, dz + 3, span] = value

    def cell(q, dz, half):
        return store.at[q, dz + 3, half] if dz else plain.at[q, half]

    def main_far(x, half):
        def far(q, d):
            return cell(q, d[2], half)[x + LEAD + d[0], LEAD + d[1] : LEAD + d[1] + 8]

        return far

    def own_far(row):
        def far(q, d):
            at = LEAD + row + d[1]
            return strip_own[q, d[0] + 3, d[2] + 3, at : at + 8]

        return far

    HERE = (0, 0, 0)

    def shifted_own(far):
        mine = [far(c, HERE) for c in range(3)]
        return [{v: (mine[c] - float(v) if v else mine[c]) for v in range(-3, 4)} for c in range(3)]

    def separation(far, mine, d):
        return [far(c, d) - mine[c][d[c]] for c in range(3)]

    def tiles(body):
        def step(x, carry):
            for half in range(2):
                body(2 * x + half, x, half)
            return carry

        lax.fori_loop(0, planes, step, 0)

    def put(r, q, field, x, half, value):
        x_of[r][0, q, 2 * x + half] = value
        plain[field, half, x + LEAD, LEAD : LEAD + rows] = value

    def window(tile_of):
        packed = jnp.zeros((8, 128), F32)
        for p in range(planes):
            both = jnp.where(lane < 64, tile_of(p, 0), tile_of(p, 1))
            moved = pltpu.roll(both, (ext + width * p) % 128, 1)
            packed = moved if p == 0 else jnp.where(lane >= width * p, moved, packed)
        return jnp.where(spot < 2 * ext, packed, pltpu.roll(packed, 2 * ext, 1))

    for load in loads[2:]:
        load.wait()
    for c in range(3):
        x_disp[0, c, n_tiles] = window(lambda p, half: x_disp[0, c, 2 * p + half])
        for bi in range(2):
            z_edge_out[bi, c] = x_disp[0, c, n_tiles, (rows - LEAD) * (1 - bi) : (rows - LEAD) * (1 - bi) + LEAD]
    pack(NEAR)
    loads[1].wait()
    for k in range(len(BONDS)):
        rest_out[k] = window(lambda p, half: rest[k, p, 0, :, half * 128 : half * 128 + 128])
    pl.semaphore_wait(barrier, n_dev - 1)
    send(NEAR)
    pack(FAR)
    send(FAR)

    loads[0].wait()

    def height_row(i, carry):
        at_x = lax.rem(gx * planes + i + nx_all - 1, nx_all)
        for row in range(rows + 2):
            at_y = lax.rem(y_tile * rows + row + ny_all - 1, ny_all)
            hb[i, LEAD - 1 + row : LEAD + row] = jnp.full((1, 128), heights[at_x, at_y], jnp.int32)
        return carry

    lax.fori_loop(0, planes + 2, height_row, 0)
    group = lane // width
    for dx in range(-1, 2):
        for band in range(2):
            packed = hb[dx + 1, 8 * band : 8 * band + 8]
            for p in range(1, planes):
                packed = jnp.where(group >= p, hb[p + dx + 1, 8 * band : 8 * band + 8], packed)
            hs[dx + 1, 8 * band : 8 * band + 8] = packed

    def own_rows(x, carry):
        for c in range(3):
            for half in range(2):
                plain[c, half, x + LEAD, LEAD : LEAD + rows] = x_disp[0, c, 2 * x + half]
        for k in range(len(BONDS)):
            for half in range(2):
                gains[k, 2 * x + half] = 10.0 / rest[k, x, 0, :, half * 128 : half * 128 + 128]
        return carry

    lax.fori_loop(0, planes, own_rows, 0)

    def count_column(i, carry):
        for j in range(ny_all):
            carry = carry + jnp.clip(heights[i, j], 0, z_tiles * cols)
        return carry

    atoms = lax.fori_loop(0, nx_all, count_column, jnp.zeros((), jnp.int32))
    receive(NEAR)
    place(NEAR, 0, 1)
    strips_of_displacement(NEAR)
    shift_main(range(3), 1, 1)
    for q in range(3):
        shift_own(q, SHIFTS_NEAR)
    for k in range(len(BONDS)):
        length = blend(rest_in[0, k], rest_out[k], rest_in[1, k])
        rest_strip[k] = length
        gains[k, n_tiles] = 10.0 / length

    def bond_sums(far, layer, height_of, length_of, gain_of, keep):
        mine = shifted_own(far)
        height = height_of(HERE)
        here = (layer >= 0) & (layer < height)
        density = jnp.zeros((8, 128), F32)
        energy = jnp.zeros((8, 128), F32)
        room = jnp.zeros((8, 128), F32)
        for k, d in enumerate(BONDS):
            s = separation(far, mine, d)
            r_sq = s[0] * s[0] + s[1] * s[1] + s[2] * s[2]
            inv_r = lax.rsqrt(r_sq)
            radius = r_sq * inv_r
            partner = (layer < height_of(d) - d[2]) & (layer >= -d[2])
            paired = partner & here
            decay = jnp.exp(3.0 - 3.0 * radius)
            cut = jnp.maximum(1.0 - r_sq * (1.0 / CUTOFF_SQ), 0.0)
            cut_value = cut * cut
            gain = gain_of(k)
            strain = (radius - length_of(k)) * gain
            squared = strain * strain
            lifted = jnp.exp(8.0 * squared)
            density = density + jnp.where(partner, decay * cut_value, 0.0)
            energy = energy + jnp.where(paired, lifted, 0.0)
            room = room + jnp.where(paired, 1.0 - squared, 0.0)
            if keep is not None:
                scale = jnp.where(paired, inv_r, 0.0)
                cut_slope = (-4.0 / CUTOFF_SQ) * radius * cut
                bonds[keep, k, 0] = scale * 0.6 * (decay * decay) * (cut_slope - 6.0 * cut_value)
                bonds[keep, k, 1] = scale * decay * (cut_slope - 3.0 * cut_value)
                strain_slope = scale * (2.0 * strain * gain)
                bonds[keep, k, 2] = strain_slope * (8.0 * lifted)
                bonds[keep, k, 3] = strain_slope
        return density, energy, room

    def main_layer(half):
        return lane + (z_tile * cols + half * 128)

    strip_layer = z_tile * cols + jnp.where(spot < 2 * ext, spot - ext, spot + (cols - width + ext))

    def main_height(x):
        return lambda d: hb[x + 1 + d[0], LEAD + d[1] : LEAD + d[1] + 8]

    def strip_height(d):
        return hs[d[0] + 1, LEAD + d[1] : LEAD + d[1] + 8]

    def embed_slope(density):
        return -0.5 * lax.rsqrt(density + 0.5)

    def bond_pass(i, x, half):
        density, energy, room = bond_sums(
            main_far(x, half),
            main_layer(half),
            main_height(x),
            lambda k: rest[k, x, 0, :, half * 128 : half * 128 + 128],
            lambda k: gains[k, i],
            i,
        )
        put(ENERGY, 0, Q_ENERGY, x, half, energy)
        put(SLOPES, 0, Q_EMBED, x, half, embed_slope(density))
        part[i, 0] = room

    tiles(bond_pass)
    density, energy, room = bond_sums(
        own_far(0), strip_layer, strip_height, lambda k: rest_strip[k], lambda k: gains[k, n_tiles], None
    )
    x_energy[0, 0, n_tiles] = energy
    x_slopes[0, 0, n_tiles] = embed_slope(density)
    part[n_tiles, 0] = room
    pack(ENERGY)
    send(ENERGY)

    receive(FAR)
    place(FAR, 0, 3)
    strips_of_displacement(FAR)
    shift_main(range(3), 3, 3)
    for q in range(3):
        shift_own(q, SHIFTS)

    def insides(far, i, keep):
        mine = shifted_own(far)
        for k, d in enumerate(REACH):
            s = separation(far, mine, d)
            r_sq = s[0] * s[0] + s[1] * s[1] + s[2] * s[2]
            inside = jnp.maximum(1.0 - r_sq * (1.0 / REACH_SQ), 0.0)
            squares[i, k] = inside * inside
            if keep:
                for c in range(3):
                    pulls[i, k, c] = inside * s[c]

    tiles(lambda i, x, half: insides(main_far(x, half), i, True))
    insides(own_far(0), n_tiles, False)
    receive(ENERGY)
    place(ENERGY, Q_ENERGY, 3)
    shift_main([Q_ENERGY], 3, 3)
    shift_own(Q_ENERGY, SHIFTS)
    first[...] = jnp.zeros_like(first)

    def tapered(q, far, i):
        sums_of = [jnp.zeros((8, 128), F32) for _ in range(4)]
        for k, d in enumerate(REACH):
            sums_of[k % 4] = sums_of[k % 4] + squares[i, k] * far(q, d)
        return (sums_of[0] + sums_of[1]) + (sums_of[2] + sums_of[3])

    def smooth(far, i, here):
        total = 1.0 + far(Q_ENERGY, HERE) + tapered(Q_ENERGY, far, i)
        room = part[i, 0]
        value = jnp.log(total) * 0.125
        share = 1.0 / (1.0 + value * value)
        gain = 0.08 * share
        adjoint = room * 0.08 * (-2.0 * value) * (share * share) / (8.0 * total)
        return jnp.where(here, adjoint, 0.0), gain, room

    def smooth_pass(i, x, half):
        here = main_layer(half) < main_height(x)(HERE)
        adjoint, gain, room = smooth(main_far(x, half), i, here)
        put(ADJOINT, 0, Q_ADJOINT, x, half, adjoint)
        put(SLOPES, 1, Q_GAIN, x, half, gain)
        first[...] += jnp.where(here, jnp.exp(gain * room * 2.0), 0.0)

    tiles(smooth_pass)
    here = (strip_layer >= 0) & (strip_layer < strip_height(HERE))
    adjoint, gain, room = smooth(own_far(0), n_tiles, here)
    x_adjoint[0, 0, n_tiles] = adjoint
    x_slopes[0, 1, n_tiles] = gain
    pack(ADJOINT)
    send(ADJOINT)
    pack(SLOPES)
    send(SLOPES)
    sums[0] = jnp.sum(first[...], axis=0, keepdims=True)

    def reduction(k):
        to = lax.rem(rank + k, n_dev)
        return pltpu.make_async_remote_copy(
            src_ref=sums.at[0],
            dst_ref=sums.at[k],
            send_sem=red_send.at[k],
            recv_sem=red_recv.at[k],
            device_id=(to // n_yz, lax.rem(to, n_yz)),
            device_id_type=MESH,
        )

    def spread(k, carry):
        reduction(k).start()
        return carry

    lax.fori_loop(1, n_dev, spread, 0)

    def energy_pull(i, x, half):
        far = main_far(x, half)
        total = [jnp.zeros((8, 128), F32) for _ in range(3)]
        for k, d in enumerate(REACH):
            energy = far(Q_ENERGY, d)
            total = [total[c] + pulls[i, k, c] * energy for c in range(3)]
        for c in range(3):
            part[i, 1 + c] = total[c]

    tiles(energy_pull)

    receive(ADJOINT)
    place(ADJOINT, Q_ADJOINT, 3)
    shift_main([Q_ADJOINT], 3, 3)
    shift_own(Q_ADJOINT, SHIFTS)

    def lambda_pass(i, x, half):
        far = main_far(x, half)
        put(LAMBDA, 0, Q_LAMBDA, x, half, far(Q_ADJOINT, HERE) + tapered(Q_ADJOINT, far, i))

    tiles(lambda_pass)
    x_lambda[0, 0, n_tiles] = own_far(0)(Q_ADJOINT, HERE) + tapered(Q_ADJOINT, own_far(0), n_tiles)
    pack(LAMBDA)
    send(LAMBDA)

    def adjoint_pull(i, x, half):
        far = main_far(x, half)
        adjoint = far(Q_ADJOINT, HERE)
        energy = far(Q_ENERGY, HERE)
        total = [jnp.zeros((8, 128), F32) for _ in range(3)]
        for k, d in enumerate(REACH):
            other = far(Q_ADJOINT, d)
            total = [total[c] + pulls[i, k, c] * other for c in range(3)]
        for c in range(3):
            part[i, 1 + c] = (-4.0 / REACH_SQ) * (adjoint * part[i, 1 + c] + energy * total[c])

    tiles(adjoint_pull)
    receive(SLOPES)
    place(SLOPES, Q_EMBED, 1)
    shift_main([Q_EMBED, Q_GAIN], 1, 1)
    receive(LAMBDA)
    place(LAMBDA, Q_LAMBDA, 1)
    shift_main([Q_LAMBDA], 1, 1)

    def final_pass(i, x, half):
        far = main_far(x, half)
        mine = shifted_own(far)
        lam, embed, gain = far(Q_LAMBDA, HERE), far(Q_EMBED, HERE), far(Q_GAIN, HERE)
        force = [part[i, 1 + c] for c in range(3)]
        for k, d in enumerate(BONDS):
            s = separation(far, mine, d)
            weight = (
                bonds[i, k, 0]
                + (embed + far(Q_EMBED, d)) * bonds[i, k, 1]
                + (lam + far(Q_LAMBDA, d)) * bonds[i, k, 2]
                - (gain + far(Q_GAIN, d)) * bonds[i, k, 3]
            )
            force = [force[c] + weight * s[c] for c in range(3)]
        span = slice(half * 128, half * 128 + 128)
        for c in range(3):
            forces[c, x, 0, :, span] = force[c]

    def collect(k, carry):
        reduction(k).wait_recv()
        return carry

    tiles(final_pass)
    lax.fori_loop(1, n_dev, collect, 0)
    total = jnp.sum(jnp.sum(sums[...], axis=0), axis=1, keepdims=True)
    boost[...] = jnp.broadcast_to(total, (1, 128)) / jnp.full((1, 128), atoms.astype(F32))

    def finish(k, carry):
        reduction(k).wait_send()
        return carry

    lax.fori_loop(1, n_dev, finish, 0)
    for r in range(len(ROUNDS)):
        for copy in copies[r]:
            copy.wait_send()


def body(n_gx, n_yz, displacement, velocity, rest_length, heights):
    _, planes, _, rows, cols = displacement.shape
    z_tiles = n_yz // (heights.shape[1] // rows)
    slots = 2 if n_gx == 2 else 3
    n_dev = n_gx * n_yz
    n_tiles = 2 * planes
    n_bonds = len(BONDS)
    n_msg = 3 + 2 * slots + 6 * slots + 2
    y_rows = [count * (n_tiles + 1) * (high - low + 1) for count, low, high in ROUNDS]
    scratch = [pltpu.VMEM((slots, count, n_tiles + 1, 8, 128), F32) for count in (3, 1, 1, 2, 1)]
    scratch += [pltpu.VMEM((2, n, 128), F32) for n in y_rows]
    scratch += [pltpu.VMEM((2, slots, n, 128), F32) for n in y_rows]
    scratch += [
        pltpu.VMEM((2, slots, 3, 8, 128), F32),
        pltpu.VMEM((2, 3, LEAD, 128), F32),
        pltpu.VMEM((2, 2, slots, 3, LEAD, 128), F32),
        pltpu.VMEM((n_bonds, 8, 128), F32),
        pltpu.VMEM((2, n_bonds, 8, 128), F32),
        pltpu.VMEM((8, 2, planes + 2 * LEAD, BAND, 128), F32),
        pltpu.VMEM((8, 2, planes + 2 * LEAD, BAND, 128), F32),
        pltpu.VMEM((8, 7, 2, planes + 2 * LEAD, BAND, 128), F32),
        pltpu.VMEM((8, slots, BAND, 128), F32),
        pltpu.VMEM((5, 7, 7, BAND, 128), F32),
        pltpu.VMEM((planes + 2, BAND, 128), jnp.int32),
        pltpu.VMEM((3, BAND, 128), jnp.int32),
        pltpu.VMEM((n_tiles + 1, len(REACH), 8, 128), F32),
        pltpu.VMEM((n_tiles, len(REACH), 3, 8, 128), F32),
        pltpu.VMEM((n_tiles, n_bonds, 4, 8, 128), F32),
        pltpu.VMEM((n_tiles + 1, 4, 8, 128), F32),
        pltpu.VMEM((8, 128), F32),
        pltpu.VMEM((n_dev, 1, 128), F32),
        pltpu.VMEM((n_bonds, n_tiles + 1, 8, 128), F32),
        pltpu.VMEM((n_bonds, 8, 128), F32),
        pltpu.VMEM(rest_length.shape, F32),
        pltpu.SMEM(heights.shape, jnp.int32),
        pltpu.SemaphoreType.DMA((len(ROUNDS), n_msg)),
        pltpu.SemaphoreType.DMA((len(ROUNDS), n_msg)),
        pltpu.SemaphoreType.DMA((n_dev,)),
        pltpu.SemaphoreType.DMA((n_dev,)),
        pltpu.SemaphoreType.DMA((2 + n_tiles,)),
    ]
    vmem = pl.BlockSpec(memory_space=pltpu.VMEM)
    hbm = pl.BlockSpec(memory_space=pltpu.HBM)
    forces, boost = pl.pallas_call(
        functools.partial(kernel, n_gx, n_yz, z_tiles),
        out_shape=(
            jax.ShapeDtypeStruct(displacement.shape, F32),
            jax.ShapeDtypeStruct((1, 128), F32),
        ),
        in_specs=[hbm, hbm, hbm],
        out_specs=(vmem, vmem),
        scratch_shapes=scratch,
        compiler_params=pltpu.CompilerParams(
            collective_id=0, has_side_effects=True, vmem_limit_bytes=64_000_000
        ),
    )(heights, displacement, rest_length)
    new_vel = velocity + 0.2 * forces
    return displacement + 0.05 * new_vel, new_vel, boost[0, 0]


def solution(mesh):
    tiled = P(None, "gx", "yz", None, None)
    sizes = (mesh.shape["gx"], mesh.shape["yz"])
    return jax.shard_map(
        functools.partial(body, *sizes),
        mesh=mesh,
        in_specs=(tiled, tiled, tiled, P()),
        out_specs=(tiled, tiled, P()),
        check_vma=False,
    )
```

```python
import functools

import jax
import jax.numpy as jnp
from jax import lax
from jax.experimental import pallas as pl
from jax.experimental.pallas import tpu as pltpu
from jax.sharding import PartitionSpec as P

CUTOFF_SQ = 1.5 * 1.5
REACH_SQ = 3.5 * 3.5
F32 = jnp.float32
MESH = pl.DeviceIdType.MESH


def list_offsets(reach_sq, forward_only):
    chosen = []
    for ax in range(-3, 4):
        for ay in range(-3, 4):
            for az in range(-3, 4):
                length_sq = ax * ax + ay * ay + az * az
                if 0 < length_sq <= reach_sq:
                    if not forward_only or (ax, ay, az) > (0, 0, 0):
                        chosen.append((ax, ay, az))
    return chosen


FORWARD = list_offsets(2, True)
BONDS = FORWARD + [(-v[0], -v[1], -v[2]) for v in FORWARD]
REACH = list_offsets(9, False)
SHIFTS = [(dx, dz) for dx in range(-3, 4) for dz in range(-3, 4) if dx * dx + dz * dz <= 9]
SHIFTS_NEAR = [(dx, dz) for dx in range(-1, 2) for dz in range(-1, 2)]

NEAR, FAR, ENERGY, ADJOINT, SLOPES, LAMBDA = range(6)
ROUNDS = [(3, 1, 1), (3, 2, 3), (1, 1, 3), (1, 1, 3), (2, 1, 1), (1, 1, 1)]
Q_ENERGY, Q_ADJOINT, Q_LAMBDA, Q_EMBED, Q_GAIN = range(3, 8)
LEAD = 4
BAND = 16


def kernel(n_gx, n_yz, z_tiles, heights_hbm, disp, rest_hbm, forces, boost, *scratch):
    (x_disp, x_energy, x_adjoint, x_slopes, x_lambda) = scratch[0:5]
    ys = scratch[5:11]
    yr = scratch[11:17]
    scratch = scratch[3:]
    (z_mid, z_edge_out, z_edge, rest_out, rest_in) = scratch[14:19]
    (plain, edges, store, strip, strip_own, hb, hs, squares, pulls, bonds, part, first, sums) = scratch[19:32]
    (gains, rest_strip, rest, heights) = scratch[32:36]
    (send_sem, recv_sem, red_send, red_recv, load_sem) = scratch[36:41]
    x_of = [x_disp, x_disp, x_energy, x_adjoint, x_slopes, x_lambda]
    nx_all, ny_all = heights.shape
    loads = [
        pltpu.make_async_copy(heights_hbm, heights, load_sem.at[0]),
        pltpu.make_async_copy(rest_hbm, rest, load_sem.at[1]),
    ]
    planes, rows, cols = disp.shape[1], disp.shape[3], disp.shape[4]
    for half in range(2):
        for p in range(planes):
            loads.append(
                pltpu.make_async_copy(
                    disp.at[:, p, 0, :, half * 128 : half * 128 + 128],
                    x_disp.at[0, :, 2 * p + half],
                    load_sem.at[2 + 2 * p + half],
                )
            )
    for load in loads[2:] + loads[:2]:
        load.start()
    n_tiles = 2 * planes
    width = 128 // planes
    ext = width // 4
    y_tiles = n_yz // z_tiles
    gx = lax.axis_index("gx")
    me = lax.axis_index("yz")
    h = me + z_tiles // 2
    y_tile = lax.rem(h // z_tiles, y_tiles)
    z_tile = lax.rem(h, z_tiles)
    x_steps = [0, 1] if n_gx == 2 else [0, 1, -1]
    n_slots = len(x_steps)
    steps = [0, 1, -1]
    left_slot, right_slot = 1, n_slots - 1

    targets = {}

    def target(a, b, c):
        if (a, b, c) not in targets:
            to_y = lax.rem(y_tile + b + y_tiles, y_tiles)
            to_z = lax.rem(z_tile + c + z_tiles, z_tiles)
            to = lax.rem(to_y * z_tiles + to_z + n_yz - z_tiles // 2, n_yz)
            targets[(a, b, c)] = (lax.rem(gx + a + n_gx, n_gx), to)
        return targets[(a, b, c)]

    n_dev = n_gx * n_yz
    rank = gx * n_yz + me
    barrier = pltpu.get_barrier_semaphore()

    def greet(k, carry):
        to = lax.rem(rank + k, n_dev)
        pl.semaphore_signal(barrier, inc=1, device_id=(to // n_yz, lax.rem(to, n_yz)), device_id_type=MESH)
        return carry

    lax.fori_loop(1, n_dev, greet, 0)

    lane = lax.broadcasted_iota(jnp.int32, (8, 128), 1)
    spot = lax.rem(lane, width)

    def x_messages(r):
        buf = x_of[r]
        top = n_tiles - 2
        if r in (NEAR, SLOPES, LAMBDA):
            out = [
                (buf.at[0, :, top : n_tiles + 1], buf.at[left_slot, :, top : n_tiles + 1], 1),
                (buf.at[0, :, 0:2], buf.at[right_slot, :, 0:2], -1),
            ]
            if n_slots == 3:
                out.append((buf.at[0, :, n_tiles], buf.at[right_slot, :, n_tiles], -1))
        elif r == FAR:
            if n_slots == 2:
                out = [(buf.at[0, :, 2:top], buf.at[1, :, 2:top], 1)]
            else:
                out = [
                    (buf.at[0, :, 0:top], buf.at[left_slot, :, 0:top], 1),
                    (buf.at[0, :, 2:n_tiles], buf.at[right_slot, :, 2:n_tiles], -1),
                ]
        else:
            out = [(buf.at[0], buf.at[ai], x_steps[ai]) for ai in range(1, n_slots)]
        return [(src, dst, a, 0, 0) for src, dst, a in out]

    def messages(r):
        out = []
        if r == NEAR:
            for ai, a in reversed(list(enumerate(x_steps))):
                for ci in range(2):
                    for bi in range(2):
                        out.append((z_edge_out.at[bi], z_edge.at[ci, bi, ai], a, steps[1 + bi], steps[1 + ci]))
                    out.append((x_disp.at[0, :, n_tiles], z_mid.at[ci, ai], a, 0, steps[1 + ci]))
        far = []
        for ai, a in reversed(list(enumerate(x_steps))):
            for bi in range(2):
                far.append((ys[r].at[bi], yr[r].at[bi, ai], a, steps[1 + bi], 0))
        out = sorted(far + out, key=lambda m: -sum(abs(v) for v in m[2:]))
        out = out + x_messages(r)
        if r == NEAR:
            for ci in range(2):
                out.append((rest_out, rest_in.at[ci], 0, 0, steps[1 + ci]))
        return [
            pltpu.make_async_remote_copy(
                src_ref=src,
                dst_ref=dst,
                send_sem=send_sem.at[r, i],
                recv_sem=recv_sem.at[r, i],
                device_id=target(a, b, c),
                device_id_type=MESH,
            )
            for i, (src, dst, a, b, c) in enumerate(out)
        ]

    copies = [messages(r) for r in range(len(ROUNDS))]

    def pack(r):
        count, low, high = ROUNDS[r]
        n_rows = high - low + 1
        for q in range(count):
            for t in range(n_tiles + 1):
                at = (q * (n_tiles + 1) + t) * n_rows
                ys[r][0, at : at + n_rows] = x_of[r][0, q, t, rows - high : rows - low + 1]
                ys[r][1, at : at + n_rows] = x_of[r][0, q, t, low - 1 : high]

    def send(r):
        for copy in copies[r][: len(copies[r]) - (2 if r == NEAR else 0)]:
            copy.start()

    def receive(r):
        for copy in copies[r][: len(copies[r]) - (2 if r == NEAR else 0)]:
            copy.wait_recv()

    def place_of(xp):
        if xp < 0:
            return left_slot, xp + planes
        if xp < planes:
            return 0, xp
        return right_slot, xp - planes

    def ghosts(r, q, t, slot):
        count, low, high = ROUNDS[r]
        n_rows = high - low + 1
        at = (q * (n_tiles + 1) + t) * n_rows
        return [
            (LEAD - high, LEAD - low + 1, yr[r][0, slot, at : at + n_rows]),
            (LEAD + rows + low - 1, LEAD + rows + high, yr[r][1, slot, at : at + n_rows]),
        ]

    def place(r, base, reach):
        for q in range(ROUNDS[r][0]):
            for xp in range(-reach, planes + reach):
                slot, plane = place_of(xp)
                at = xp + LEAD
                for half in range(2):
                    t = 2 * plane + half
                    if slot:
                        plain[base + q, half, at, LEAD : LEAD + rows] = x_of[r][slot, q, t]
                    for lo, hi, value in ghosts(r, q, t, slot) + (ghosts(NEAR, q, t, slot) if r == FAR else []):
                        plain[base + q, half, at, lo:hi] = value
            for slot in range(n_slots):
                if r != NEAR and r != FAR:
                    strip[base + q, slot, LEAD : LEAD + rows] = x_of[r][slot, q, n_tiles]
                    for lo, hi, value in ghosts(r, q, n_tiles, slot):
                        strip[base + q, slot, lo:hi] = value

    def blend(below, own, above):
        return jnp.where(spot < ext, below, jnp.where(spot >= width - ext, above, own))

    def strips_of_displacement(r):
        lane4 = lane[0:4]
        for q in range(3):
            for slot in range(n_slots):
                if r == NEAR:
                    strip[q, slot, LEAD : LEAD + rows] = blend(z_mid[0, slot, q], x_disp[slot, q, n_tiles], z_mid[1, slot, q])
                for bi, (lo, hi, value) in enumerate(ghosts(r, q, n_tiles, slot)):
                    first_row = lo - (0 if bi == 0 else LEAD + rows)
                    span = slice(first_row, first_row + hi - lo)
                    n = hi - lo
                    spot_n = spot[0:n]
                    strip[q, slot, lo:hi] = jnp.where(
                        spot_n < ext,
                        z_edge[0, bi, slot, q, span],
                        jnp.where(spot_n >= width - ext, z_edge[1, bi, slot, q, span], value),
                    )

    def shift_main(fields, reach, depth):
        inner = min(reach, max(1, reach - 1))
        spans = []
        for q in fields:
            for xp in range(-inner, planes + inner):
                for band in range(2):
                    spans.append((q, xp, band, slice(8 * band, 8 * band + 8)))
        for q, xp, band, span in spans:
            slot, plane = place_of(xp)
            edge = strip[q, slot, span]
            edges[q, 0, xp + LEAD, span] = pltpu.roll(edge, (128 - ext - width * plane) % 128, 1)
            edges[q, 1, xp + LEAD, span] = pltpu.roll(edge, (ext - width * plane - width) % 128, 1)
        for q, xp, band, span in spans:
            at = xp + LEAD
            t1 = plain[q, 0, at, span]
            t2 = plain[q, 1, at, span]
            low = edges[q, 0, at, span]
            high = edges[q, 1, at, span]
            for dz in range(1, depth + 1):
                if dz == 3 and not 3 - reach <= xp < planes + reach - 3:
                    continue
                up = lane < dz
                down = lane >= 128 - dz
                store[q, 3 + dz, 0, at, span] = pltpu.roll(jnp.where(up, t2, t1), 128 - dz, 1)
                store[q, 3 + dz, 1, at, span] = pltpu.roll(jnp.where(up, high, t2), 128 - dz, 1)
                store[q, 3 - dz, 0, at, span] = pltpu.roll(jnp.where(down, low, t1), dz, 1)
                store[q, 3 - dz, 1, at, span] = pltpu.roll(jnp.where(down, t1, t2), dz, 1)

    def shift_own(q, shifts):
        for band in range(2):
            span = slice(8 * band, 8 * band + 8)
            own, left, right = strip[q, 0, span], strip[q, left_slot, span], strip[q, right_slot, span]
            for dx, dz in shifts:
                s = width * dx + dz
                if s > 0:
                    value = pltpu.roll(jnp.where(lane >= s, own, right), 128 - s, 1)
                elif s < 0:
                    value = pltpu.roll(jnp.where(lane < 128 + s, own, left), -s, 1)
                else:
                    value = own
                strip_own[q, dx + 3, dz + 3, span] = value

    def cell(q, dz, half):
        return store.at[q, dz + 3, half] if dz else plain.at[q, half]

    def main_far(x, half):
        def far(q, d):
            return cell(q, d[2], half)[x + LEAD + d[0], LEAD + d[1] : LEAD + d[1] + 8]

        return far

    def own_far(row):
        def far(q, d):
            at = LEAD + row + d[1]
            return strip_own[q, d[0] + 3, d[2] + 3, at : at + 8]

        return far

    HERE = (0, 0, 0)

    def shifted_own(far):
        mine = [far(c, HERE) for c in range(3)]
        return [{v: (mine[c] - float(v) if v else mine[c]) for v in range(-3, 4)} for c in range(3)]

    def separation(far, mine, d):
        return [far(c, d) - mine[c][d[c]] for c in range(3)]

    def tiles(body):
        def step(x, carry):
            for half in range(2):
                body(2 * x + half, x, half)
            return carry

        lax.fori_loop(0, planes, step, 0)

    def each_tile(body):
        for i in range(n_tiles):
            body(i, i // 2, i % 2)

    def put(r, q, field, x, half, value):
        x_of[r][0, q, 2 * x + half] = value
        plain[field, half, x + LEAD, LEAD : LEAD + rows] = value

    def window(tile_of):
        packed = jnp.zeros((8, 128), F32)
        for p in range(planes):
            both = jnp.where(lane < 64, tile_of(p, 0), tile_of(p, 1))
            moved = pltpu.roll(both, (ext + width * p) % 128, 1)
            packed = moved if p == 0 else jnp.where(lane >= width * p, moved, packed)
        return jnp.where(spot < 2 * ext, packed, pltpu.roll(packed, 2 * ext, 1))

    for load in loads[2:]:
        load.wait()
    for c in range(3):
        x_disp[0, c, n_tiles] = window(lambda p, half: x_disp[0, c, 2 * p + half])
        for bi in range(2):
            z_edge_out[bi, c] = x_disp[0, c, n_tiles, (rows - LEAD) * (1 - bi) : (rows - LEAD) * (1 - bi) + LEAD]
    pack(NEAR)
    pl.semaphore_wait(barrier, n_dev - 1)
    send(NEAR)
    loads[1].wait()
    for k in range(len(BONDS)):
        rest_out[k] = window(lambda p, half: rest[k, p, 0, :, half * 128 : half * 128 + 128])
    for copy in copies[NEAR][-2:]:
        copy.start()
    pack(FAR)
    send(FAR)

    loads[0].wait()

    def height_row(i, carry):
        at_x = lax.rem(gx * planes + i + nx_all - 1, nx_all)
        for row in range(rows + 2):
            at_y = lax.rem(y_tile * rows + row + ny_all - 1, ny_all)
            hb[i, LEAD - 1 + row : LEAD + row] = jnp.full((1, 128), heights[at_x, at_y], jnp.int32)
        return carry

    lax.fori_loop(0, planes + 2, height_row, 0)
    group = lane // width
    for dx in range(-1, 2):
        for band in range(2):
            packed = hb[dx + 1, 8 * band : 8 * band + 8]
            for p in range(1, planes):
                packed = jnp.where(group >= p, hb[p + dx + 1, 8 * band : 8 * band + 8], packed)
            hs[dx + 1, 8 * band : 8 * band + 8] = packed

    def own_rows(x, carry):
        for c in range(3):
            for half in range(2):
                plain[c, half, x + LEAD, LEAD : LEAD + rows] = x_disp[0, c, 2 * x + half]
        for k in range(len(BONDS)):
            for half in range(2):
                gains[k, 2 * x + half] = 10.0 / rest[k, x, 0, :, half * 128 : half * 128 + 128]
        return carry

    lax.fori_loop(0, planes, own_rows, 0)

    def count_column(i, carry):
        for j in range(ny_all):
            carry = carry + jnp.clip(heights[i, j], 0, z_tiles * cols)
        return carry

    atoms = lax.fori_loop(0, nx_all, count_column, jnp.zeros((), jnp.int32))
    receive(NEAR)
    place(NEAR, 0, 1)
    strips_of_displacement(NEAR)
    shift_main(range(3), 1, 1)
    for q in range(3):
        shift_own(q, SHIFTS_NEAR)

    def bond_sums(far, layer, height_of, length_of, gain_of, keep):
        mine = shifted_own(far)
        height = height_of(HERE)
        here = (layer >= 0) & (layer < height)
        density = jnp.zeros((8, 128), F32)
        energy = jnp.zeros((8, 128), F32)
        room = jnp.zeros((8, 128), F32)
        for k, d in enumerate(BONDS):
            s = separation(far, mine, d)
            r_sq = s[0] * s[0] + s[1] * s[1] + s[2] * s[2]
            inv_r = lax.rsqrt(r_sq)
            radius = r_sq * inv_r
            partner = (layer < height_of(d) - d[2]) & (layer >= -d[2])
            paired = partner & here
            decay = jnp.exp(3.0 - 3.0 * radius)
            cut = jnp.maximum(1.0 - r_sq * (1.0 / CUTOFF_SQ), 0.0)
            cut_value = cut * cut
            gain = gain_of(k)
            strain = (radius - length_of(k)) * gain
            squared = strain * strain
            lifted = jnp.exp(8.0 * squared)
            density = density + jnp.where(partner, decay * cut_value, 0.0)
            energy = energy + jnp.where(paired, lifted, 0.0)
            room = room + jnp.where(paired, 1.0 - squared, 0.0)
            if keep is not None:
                scale = jnp.where(paired, inv_r, 0.0)
                cut_slope = (-4.0 / CUTOFF_SQ) * radius * cut
                bonds[keep, k, 0] = scale * 0.6 * (decay * decay) * (cut_slope - 6.0 * cut_value)
                bonds[keep, k, 1] = scale * decay * (cut_slope - 3.0 * cut_value)
                strain_slope = scale * (2.0 * strain * gain)
                bonds[keep, k, 2] = strain_slope * (8.0 * lifted)
                bonds[keep, k, 3] = strain_slope
        return density, energy, room

    def main_layer(half):
        return lane + (z_tile * cols + half * 128)

    strip_layer = z_tile * cols + jnp.where(spot < 2 * ext, spot - ext, spot + (cols - width + ext))

    def main_height(x):
        return lambda d: hb[x + 1 + d[0], LEAD + d[1] : LEAD + d[1] + 8]

    def strip_height(d):
        return hs[d[0] + 1, LEAD + d[1] : LEAD + d[1] + 8]

    def embed_slope(density):
        return -0.5 * lax.rsqrt(density + 0.5)

    def bond_pass(i, x, half):
        density, energy, room = bond_sums(
            main_far(x, half),
            main_layer(half),
            main_height(x),
            lambda k: rest[k, x, 0, :, half * 128 : half * 128 + 128],
            lambda k: gains[k, i],
            i,
        )
        put(ENERGY, 0, Q_ENERGY, x, half, energy)
        put(SLOPES, 0, Q_EMBED, x, half, embed_slope(density))
        part[i, 0] = room

    tiles(bond_pass)
    for copy in copies[NEAR][-2:]:
        copy.wait_recv()
    for k in range(len(BONDS)):
        length = blend(rest_in[0, k], rest_out[k], rest_in[1, k])
        rest_strip[k] = length
        gains[k, n_tiles] = 10.0 / length
    density, energy, room = bond_sums(
        own_far(0), strip_layer, strip_height, lambda k: rest_strip[k], lambda k: gains[k, n_tiles], None
    )
    x_energy[0, 0, n_tiles] = energy
    x_slopes[0, 0, n_tiles] = embed_slope(density)
    part[n_tiles, 0] = room
    pack(ENERGY)
    send(ENERGY)

    receive(FAR)
    place(FAR, 0, 3)
    strips_of_displacement(FAR)
    shift_main(range(3), 3, 3)
    for q in range(3):
        shift_own(q, SHIFTS)

    def insides(far, i, keep):
        mine = shifted_own(far)
        for k, d in enumerate(REACH):
            s = separation(far, mine, d)
            r_sq = s[0] * s[0] + s[1] * s[1] + s[2] * s[2]
            inside = jnp.maximum(1.0 - r_sq * (1.0 / REACH_SQ), 0.0)
            squares[i, k] = inside * inside
            if keep:
                for c in range(3):
                    pulls[i, k, c] = inside * s[c]

    tiles(lambda i, x, half: insides(main_far(x, half), i, True))
    insides(own_far(0), n_tiles, False)
    receive(ENERGY)
    place(ENERGY, Q_ENERGY, 3)
    shift_main([Q_ENERGY], 3, 3)
    shift_own(Q_ENERGY, SHIFTS)
    first[...] = jnp.zeros_like(first)

    def tapered(q, far, i):
        sums_of = [jnp.zeros((8, 128), F32) for _ in range(4)]
        for k, d in enumerate(REACH):
            sums_of[k % 4] = sums_of[k % 4] + squares[i, k] * far(q, d)
        return (sums_of[0] + sums_of[1]) + (sums_of[2] + sums_of[3])

    def smooth(far, i, here):
        total = 1.0 + far(Q_ENERGY, HERE) + tapered(Q_ENERGY, far, i)
        room = part[i, 0]
        value = jnp.log(total) * 0.125
        share = 1.0 / (1.0 + value * value)
        gain = 0.08 * share
        adjoint = room * 0.08 * (-2.0 * value) * (share * share) / (8.0 * total)
        return jnp.where(here, adjoint, 0.0), gain, room

    def smooth_pass(i, x, half):
        here = main_layer(half) < main_height(x)(HERE)
        adjoint, gain, room = smooth(main_far(x, half), i, here)
        put(ADJOINT, 0, Q_ADJOINT, x, half, adjoint)
        put(SLOPES, 1, Q_GAIN, x, half, gain)
        first[...] += jnp.where(here, jnp.exp(gain * room * 2.0), 0.0)

    each_tile(smooth_pass)
    here = (strip_layer >= 0) & (strip_layer < strip_height(HERE))
    adjoint, gain, room = smooth(own_far(0), n_tiles, here)
    x_adjoint[0, 0, n_tiles] = adjoint
    x_slopes[0, 1, n_tiles] = gain
    pack(ADJOINT)
    send(ADJOINT)
    pack(SLOPES)
    send(SLOPES)
    sums[0] = jnp.sum(first[...], axis=0, keepdims=True)

    def reduction(k):
        to = lax.rem(rank + k, n_dev)
        return pltpu.make_async_remote_copy(
            src_ref=sums.at[0],
            dst_ref=sums.at[k],
            send_sem=red_send.at[k],
            recv_sem=red_recv.at[k],
            device_id=(to // n_yz, lax.rem(to, n_yz)),
            device_id_type=MESH,
        )

    def spread(k, carry):
        reduction(k).start()
        return carry

    lax.fori_loop(1, n_dev, spread, 0)

    def energy_pull(i, x, half):
        far = main_far(x, half)
        total = [jnp.zeros((8, 128), F32) for _ in range(3)]
        for k, d in enumerate(REACH):
            energy = far(Q_ENERGY, d)
            total = [total[c] + pulls[i, k, c] * energy for c in range(3)]
        for c in range(3):
            part[i, 1 + c] = total[c]

    tiles(energy_pull)

    receive(ADJOINT)
    place(ADJOINT, Q_ADJOINT, 3)
    shift_main([Q_ADJOINT], 3, 3)
    shift_own(Q_ADJOINT, SHIFTS)

    def lambda_pass(i, x, half):
        far = main_far(x, half)
        put(LAMBDA, 0, Q_LAMBDA, x, half, far(Q_ADJOINT, HERE) + tapered(Q_ADJOINT, far, i))

    each_tile(lambda_pass)
    x_lambda[0, 0, n_tiles] = own_far(0)(Q_ADJOINT, HERE) + tapered(Q_ADJOINT, own_far(0), n_tiles)
    pack(LAMBDA)
    send(LAMBDA)

    def adjoint_pull(i, x, half):
        far = main_far(x, half)
        adjoint = far(Q_ADJOINT, HERE)
        energy = far(Q_ENERGY, HERE)
        total = [jnp.zeros((8, 128), F32) for _ in range(3)]
        for k, d in enumerate(REACH):
            other = far(Q_ADJOINT, d)
            total = [total[c] + pulls[i, k, c] * other for c in range(3)]
        for c in range(3):
            part[i, 1 + c] = (-4.0 / REACH_SQ) * (adjoint * part[i, 1 + c] + energy * total[c])

    tiles(adjoint_pull)
    receive(SLOPES)
    place(SLOPES, Q_EMBED, 1)
    shift_main([Q_EMBED, Q_GAIN], 1, 1)

    def collect(k, carry):
        reduction(k).wait_recv()
        return carry

    lax.fori_loop(1, n_dev, collect, 0)
    total = jnp.sum(jnp.sum(sums[...], axis=0), axis=1, keepdims=True)
    boost[...] = jnp.broadcast_to(total, (1, 128)) / jnp.full((1, 128), atoms.astype(F32))

    def finish(k, carry):
        reduction(k).wait_send()
        return carry

    lax.fori_loop(1, n_dev, finish, 0)
    for r in range(LAMBDA):
        for copy in copies[r]:
            copy.wait_send()
    receive(LAMBDA)
    place(LAMBDA, Q_LAMBDA, 1)
    shift_main([Q_LAMBDA], 1, 1)

    def final_pass(i, x, half):
        far = main_far(x, half)
        mine = shifted_own(far)
        lam, embed, gain = far(Q_LAMBDA, HERE), far(Q_EMBED, HERE), far(Q_GAIN, HERE)
        force = [part[i, 1 + c] for c in range(3)]
        for k, d in enumerate(BONDS):
            s = separation(far, mine, d)
            weight = (
                bonds[i, k, 0]
                + (embed + far(Q_EMBED, d)) * bonds[i, k, 1]
                + (lam + far(Q_LAMBDA, d)) * bonds[i, k, 2]
                - (gain + far(Q_GAIN, d)) * bonds[i, k, 3]
            )
            force = [force[c] + weight * s[c] for c in range(3)]
        span = slice(half * 128, half * 128 + 128)
        for c in range(3):
            forces[c, x, 0, :, span] = force[c]

    each_tile(final_pass)
    for copy in copies[LAMBDA]:
        copy.wait_send()


def body(n_gx, n_yz, displacement, velocity, rest_length, heights):
    _, planes, _, rows, cols = displacement.shape
    z_tiles = n_yz // (heights.shape[1] // rows)
    slots = 2 if n_gx == 2 else 3
    n_dev = n_gx * n_yz
    n_tiles = 2 * planes
    n_bonds = len(BONDS)
    n_msg = 3 + 2 * slots + 6 * slots + 2
    y_rows = [count * (n_tiles + 1) * (high - low + 1) for count, low, high in ROUNDS]
    scratch = [pltpu.VMEM((slots, count, n_tiles + 1, 8, 128), F32) for count in (3, 1, 1, 2, 1)]
    scratch += [pltpu.VMEM((2, n, 128), F32) for n in y_rows]
    scratch += [pltpu.VMEM((2, slots, n, 128), F32) for n in y_rows]
    scratch += [
        pltpu.VMEM((2, slots, 3, 8, 128), F32),
        pltpu.VMEM((2, 3, LEAD, 128), F32),
        pltpu.VMEM((2, 2, slots, 3, LEAD, 128), F32),
        pltpu.VMEM((n_bonds, 8, 128), F32),
        pltpu.VMEM((2, n_bonds, 8, 128), F32),
        pltpu.VMEM((8, 2, planes + 2 * LEAD, BAND, 128), F32),
        pltpu.VMEM((8, 2, planes + 2 * LEAD, BAND, 128), F32),
        pltpu.VMEM((8, 7, 2, planes + 2 * LEAD, BAND, 128), F32),
        pltpu.VMEM((8, slots, BAND, 128), F32),
        pltpu.VMEM((5, 7, 7, BAND, 128), F32),
        pltpu.VMEM((planes + 2, BAND, 128), jnp.int32),
        pltpu.VMEM((3, BAND, 128), jnp.int32),
        pltpu.VMEM((n_tiles + 1, len(REACH), 8, 128), F32),
        pltpu.VMEM((n_tiles, len(REACH), 3, 8, 128), F32),
        pltpu.VMEM((n_tiles, n_bonds, 4, 8, 128), F32),
        pltpu.VMEM((n_tiles + 1, 4, 8, 128), F32),
        pltpu.VMEM((8, 128), F32),
        pltpu.VMEM((n_dev, 1, 128), F32),
        pltpu.VMEM((n_bonds, n_tiles + 1, 8, 128), F32),
        pltpu.VMEM((n_bonds, 8, 128), F32),
        pltpu.VMEM(rest_length.shape, F32),
        pltpu.SMEM(heights.shape, jnp.int32),
        pltpu.SemaphoreType.DMA((len(ROUNDS), n_msg)),
        pltpu.SemaphoreType.DMA((len(ROUNDS), n_msg)),
        pltpu.SemaphoreType.DMA((n_dev,)),
        pltpu.SemaphoreType.DMA((n_dev,)),
        pltpu.SemaphoreType.DMA((2 + n_tiles,)),
    ]
    vmem = pl.BlockSpec(memory_space=pltpu.VMEM)
    hbm = pl.BlockSpec(memory_space=pltpu.HBM)
    forces, boost = pl.pallas_call(
        functools.partial(kernel, n_gx, n_yz, z_tiles),
        out_shape=(
            jax.ShapeDtypeStruct(displacement.shape, F32),
            jax.ShapeDtypeStruct((1, 128), F32),
        ),
        in_specs=[hbm, hbm, hbm],
        out_specs=(vmem, vmem),
        scratch_shapes=scratch,
        compiler_params=pltpu.CompilerParams(
            collective_id=0, has_side_effects=True, vmem_limit_bytes=64_000_000
        ),
    )(heights, displacement, rest_length)
    new_vel = velocity + 0.2 * forces
    return displacement + 0.05 * new_vel, new_vel, boost[0, 0]


def solution(mesh):
    tiled = P(None, "gx", "yz", None, None)
    sizes = (mesh.shape["gx"], mesh.shape["yz"])
    return jax.shard_map(
        functools.partial(body, *sizes),
        mesh=mesh,
        in_specs=(tiled, tiled, tiled, P()),
        out_specs=(tiled, tiled, P()),
        check_vma=False,
    )
```

```python
import functools

import jax
import jax.numpy as jnp
from jax import lax
from jax.experimental import pallas as pl
from jax.experimental.pallas import tpu as pltpu
from jax.sharding import PartitionSpec as P

CUTOFF_SQ = 1.5 * 1.5
REACH_SQ = 3.5 * 3.5
F32 = jnp.float32
MESH = pl.DeviceIdType.MESH


def list_offsets(reach_sq, forward_only):
    chosen = []
    for ax in range(-3, 4):
        for ay in range(-3, 4):
            for az in range(-3, 4):
                length_sq = ax * ax + ay * ay + az * az
                if 0 < length_sq <= reach_sq:
                    if not forward_only or (ax, ay, az) > (0, 0, 0):
                        chosen.append((ax, ay, az))
    return chosen


FORWARD = list_offsets(2, True)
BONDS = FORWARD + [(-v[0], -v[1], -v[2]) for v in FORWARD]
REACH = list_offsets(9, False)
SHIFTS = [(dx, dz) for dx in range(-3, 4) for dz in range(-3, 4) if dx * dx + dz * dz <= 9]
SHIFTS_NEAR = [(dx, dz) for dx in range(-1, 2) for dz in range(-1, 2)]

NEAR, FAR, ENERGY, ADJOINT, SLOPES, LAMBDA = range(6)
ROUNDS = [(3, 1, 1), (3, 2, 3), (1, 1, 3), (1, 1, 3), (2, 1, 1), (1, 1, 1)]
Q_ENERGY, Q_ADJOINT, Q_LAMBDA, Q_EMBED, Q_GAIN = range(3, 8)
LEAD = 4
BAND = 16


def kernel(n_gx, n_yz, z_tiles, heights_hbm, disp, rest_hbm, forces, boost, *scratch):
    (x_disp, x_energy, x_adjoint, x_slopes, x_lambda) = scratch[0:5]
    ys = scratch[5:11]
    yr = scratch[11:17]
    scratch = scratch[3:]
    (z_mid, z_edge_out, z_edge, rest_out, rest_in) = scratch[14:19]
    (plain, edges, store, strip, strip_own, hb, hs, squares, pulls, bonds, part, first, sums) = scratch[19:32]
    (gains, rest_strip, rest, heights) = scratch[32:36]
    (send_sem, recv_sem, red_send, red_recv, load_sem) = scratch[36:41]
    x_of = [x_disp, x_disp, x_energy, x_adjoint, x_slopes, x_lambda]
    nx_all, ny_all = heights.shape
    loads = [
        pltpu.make_async_copy(heights_hbm, heights, load_sem.at[0]),
        pltpu.make_async_copy(rest_hbm, rest, load_sem.at[1]),
    ]
    planes, rows, cols = disp.shape[1], disp.shape[3], disp.shape[4]
    for half in range(2):
        for p in range(planes):
            loads.append(
                pltpu.make_async_copy(
                    disp.at[:, p, 0, :, half * 128 : half * 128 + 128],
                    x_disp.at[0, :, 2 * p + half],
                    load_sem.at[2 + 2 * p + half],
                )
            )
    for load in loads[2:] + loads[:2]:
        load.start()
    n_tiles = 2 * planes
    width = 128 // planes
    ext = width // 4
    y_tiles = n_yz // z_tiles
    gx = lax.axis_index("gx")
    me = lax.axis_index("yz")
    h = me + z_tiles // 2
    y_tile = lax.rem(h // z_tiles, y_tiles)
    z_tile = lax.rem(h, z_tiles)
    x_steps = [0, 1] if n_gx == 2 else [0, 1, -1]
    n_slots = len(x_steps)
    steps = [0, 1, -1]
    left_slot, right_slot = 1, n_slots - 1

    targets = {}

    def target(a, b, c):
        if (a, b, c) not in targets:
            to_y = lax.rem(y_tile + b + y_tiles, y_tiles)
            to_z = lax.rem(z_tile + c + z_tiles, z_tiles)
            to = lax.rem(to_y * z_tiles + to_z + n_yz - z_tiles // 2, n_yz)
            targets[(a, b, c)] = (lax.rem(gx + a + n_gx, n_gx), to)
        return targets[(a, b, c)]

    n_dev = n_gx * n_yz
    rank = gx * n_yz + me
    barrier = pltpu.get_barrier_semaphore()

    def greet(k, carry):
        to = lax.rem(rank + k, n_dev)
        pl.semaphore_signal(barrier, inc=1, device_id=(to // n_yz, lax.rem(to, n_yz)), device_id_type=MESH)
        return carry

    lax.fori_loop(1, n_dev, greet, 0)

    lane = lax.broadcasted_iota(jnp.int32, (8, 128), 1)
    spot = lax.rem(lane, width)

    def x_messages(r):
        buf = x_of[r]
        top = n_tiles - 2
        if r in (NEAR, SLOPES, LAMBDA):
            out = [
                (buf.at[0, :, top : n_tiles + 1], buf.at[left_slot, :, top : n_tiles + 1], 1),
                (buf.at[0, :, 0:2], buf.at[right_slot, :, 0:2], -1),
            ]
            if n_slots == 3:
                out.append((buf.at[0, :, n_tiles], buf.at[right_slot, :, n_tiles], -1))
        elif r == FAR:
            if n_slots == 2:
                out = [(buf.at[0, :, 2:top], buf.at[1, :, 2:top], 1)]
            else:
                out = [
                    (buf.at[0, :, 0:top], buf.at[left_slot, :, 0:top], 1),
                    (buf.at[0, :, 2:n_tiles], buf.at[right_slot, :, 2:n_tiles], -1),
                ]
        else:
            out = [(buf.at[0], buf.at[ai], x_steps[ai]) for ai in range(1, n_slots)]
        return [(src, dst, a, 0, 0) for src, dst, a in out]

    def messages(r):
        out = []
        if r == NEAR:
            for ai, a in reversed(list(enumerate(x_steps))):
                for ci in range(2):
                    for bi in range(2):
                        out.append((z_edge_out.at[bi], z_edge.at[ci, bi, ai], a, steps[1 + bi], steps[1 + ci]))
                    out.append((x_disp.at[0, :, n_tiles], z_mid.at[ci, ai], a, 0, steps[1 + ci]))
        far = []
        for ai, a in reversed(list(enumerate(x_steps))):
            for bi in range(2):
                far.append((ys[r].at[bi], yr[r].at[bi, ai], a, steps[1 + bi], 0))
        out = sorted(far + out, key=lambda m: -sum(abs(v) for v in m[2:]))
        out = out + x_messages(r)
        if r == NEAR:
            for ci in range(2):
                out.append((rest_out, rest_in.at[ci], 0, 0, steps[1 + ci]))
        return [
            pltpu.make_async_remote_copy(
                src_ref=src,
                dst_ref=dst,
                send_sem=send_sem.at[r, i],
                recv_sem=recv_sem.at[r, i],
                device_id=target(a, b, c),
                device_id_type=MESH,
            )
            for i, (src, dst, a, b, c) in enumerate(out)
        ]

    copies = [messages(r) for r in range(len(ROUNDS))]

    def pack(r):
        count, low, high = ROUNDS[r]
        n_rows = high - low + 1
        for q in range(count):
            for t in range(n_tiles + 1):
                at = (q * (n_tiles + 1) + t) * n_rows
                ys[r][0, at : at + n_rows] = x_of[r][0, q, t, rows - high : rows - low + 1]
                ys[r][1, at : at + n_rows] = x_of[r][0, q, t, low - 1 : high]

    def send(r):
        for copy in copies[r][: len(copies[r]) - (2 if r == NEAR else 0)]:
            copy.start()

    def receive(r):
        for copy in copies[r][: len(copies[r]) - (2 if r == NEAR else 0)]:
            copy.wait_recv()

    def place_of(xp):
        if xp < 0:
            return left_slot, xp + planes
        if xp < planes:
            return 0, xp
        return right_slot, xp - planes

    def ghosts(r, q, t, slot):
        count, low, high = ROUNDS[r]
        n_rows = high - low + 1
        at = (q * (n_tiles + 1) + t) * n_rows
        return [
            (LEAD - high, LEAD - low + 1, yr[r][0, slot, at : at + n_rows]),
            (LEAD + rows + low - 1, LEAD + rows + high, yr[r][1, slot, at : at + n_rows]),
        ]

    def place(r, base, reach):
        for q in range(ROUNDS[r][0]):
            for xp in range(-reach, planes + reach):
                slot, plane = place_of(xp)
                at = xp + LEAD
                for half in range(2):
                    t = 2 * plane + half
                    if slot:
                        plain[base + q, half, at, LEAD : LEAD + rows] = x_of[r][slot, q, t]
                    for lo, hi, value in ghosts(r, q, t, slot) + (ghosts(NEAR, q, t, slot) if r == FAR else []):
                        plain[base + q, half, at, lo:hi] = value
            for slot in range(n_slots):
                if r != NEAR and r != FAR:
                    strip[base + q, slot, LEAD : LEAD + rows] = x_of[r][slot, q, n_tiles]
                    for lo, hi, value in ghosts(r, q, n_tiles, slot):
                        strip[base + q, slot, lo:hi] = value

    def blend(below, own, above):
        return jnp.where(spot < ext, below, jnp.where(spot >= width - ext, above, own))

    def strips_of_displacement(r):
        lane4 = lane[0:4]
        for q in range(3):
            for slot in range(n_slots):
                if r == NEAR:
                    strip[q, slot, LEAD : LEAD + rows] = blend(z_mid[0, slot, q], x_disp[slot, q, n_tiles], z_mid[1, slot, q])
                for bi, (lo, hi, value) in enumerate(ghosts(r, q, n_tiles, slot)):
                    first_row = lo - (0 if bi == 0 else LEAD + rows)
                    span = slice(first_row, first_row + hi - lo)
                    n = hi - lo
                    spot_n = spot[0:n]
                    strip[q, slot, lo:hi] = jnp.where(
                        spot_n < ext,
                        z_edge[0, bi, slot, q, span],
                        jnp.where(spot_n >= width - ext, z_edge[1, bi, slot, q, span], value),
                    )

    def shift_main(fields, reach, depth):
        inner = min(reach, max(1, reach - 1))
        spans = []
        for q in fields:
            for xp in range(-inner, planes + inner):
                for band in range(2):
                    spans.append((q, xp, band, slice(8 * band, 8 * band + 8)))
        for q, xp, band, span in spans:
            slot, plane = place_of(xp)
            edge = strip[q, slot, span]
            edges[q, 0, xp + LEAD, span] = pltpu.roll(edge, (128 - ext - width * plane) % 128, 1)
            edges[q, 1, xp + LEAD, span] = pltpu.roll(edge, (ext - width * plane - width) % 128, 1)
        for q, xp, band, span in spans:
            at = xp + LEAD
            t1 = plain[q, 0, at, span]
            t2 = plain[q, 1, at, span]
            low = edges[q, 0, at, span]
            high = edges[q, 1, at, span]
            for dz in range(1, depth + 1):
                if dz == 3 and not 3 - reach <= xp < planes + reach - 3:
                    continue
                up = lane < dz
                down = lane >= 128 - dz
                store[q, 3 + dz, 0, at, span] = pltpu.roll(jnp.where(up, t2, t1), 128 - dz, 1)
                store[q, 3 + dz, 1, at, span] = pltpu.roll(jnp.where(up, high, t2), 128 - dz, 1)
                store[q, 3 - dz, 0, at, span] = pltpu.roll(jnp.where(down, low, t1), dz, 1)
                store[q, 3 - dz, 1, at, span] = pltpu.roll(jnp.where(down, t1, t2), dz, 1)

    def shift_own(q, shifts):
        for band in range(2):
            span = slice(8 * band, 8 * band + 8)
            own, left, right = strip[q, 0, span], strip[q, left_slot, span], strip[q, right_slot, span]
            for dx, dz in shifts:
                s = width * dx + dz
                if s > 0:
                    value = pltpu.roll(jnp.where(lane >= s, own, right), 128 - s, 1)
                elif s < 0:
                    value = pltpu.roll(jnp.where(lane < 128 + s, own, left), -s, 1)
                else:
                    value = own
                strip_own[q, dx + 3, dz + 3, span] = value

    def cell(q, dz, half):
        return store.at[q, dz + 3, half] if dz else plain.at[q, half]

    def main_far(x, half):
        def far(q, d):
            return cell(q, d[2], half)[x + LEAD + d[0], LEAD + d[1] : LEAD + d[1] + 8]

        return far

    def own_far(row):
        def far(q, d):
            at = LEAD + row + d[1]
            return strip_own[q, d[0] + 3, d[2] + 3, at : at + 8]

        return far

    HERE = (0, 0, 0)

    def shifted_own(far):
        mine = [far(c, HERE) for c in range(3)]
        return [{v: (mine[c] - float(v) if v else mine[c]) for v in range(-3, 4)} for c in range(3)]

    def separation(far, mine, d):
        return [far(c, d) - mine[c][d[c]] for c in range(3)]

    def tiles(body):
        def step(x, carry):
            for half in range(2):
                body(2 * x + half, x, half)
            return carry

        lax.fori_loop(0, planes, step, 0)

    def each_tile(body):
        for i in range(n_tiles):
            body(i, i // 2, i % 2)

    def put(r, q, field, x, half, value):
        x_of[r][0, q, 2 * x + half] = value
        plain[field, half, x + LEAD, LEAD : LEAD + rows] = value

    def window(tile_of):
        packed = jnp.zeros((8, 128), F32)
        for p in range(planes):
            both = jnp.where(lane < 64, tile_of(p, 0), tile_of(p, 1))
            moved = pltpu.roll(both, (ext + width * p) % 128, 1)
            packed = moved if p == 0 else jnp.where(lane >= width * p, moved, packed)
        return jnp.where(spot < 2 * ext, packed, pltpu.roll(packed, 2 * ext, 1))

    for load in loads[2:]:
        load.wait()
    for c in range(3):
        x_disp[0, c, n_tiles] = window(lambda p, half: x_disp[0, c, 2 * p + half])
        for bi in range(2):
            z_edge_out[bi, c] = x_disp[0, c, n_tiles, (rows - LEAD) * (1 - bi) : (rows - LEAD) * (1 - bi) + LEAD]
    pack(NEAR)
    pl.semaphore_wait(barrier, n_dev - 1)
    send(NEAR)
    loads[1].wait()
    for k in range(len(BONDS)):
        rest_out[k] = window(lambda p, half: rest[k, p, 0, :, half * 128 : half * 128 + 128])
    for copy in copies[NEAR][-2:]:
        copy.start()
    pack(FAR)
    send(FAR)

    loads[0].wait()

    def height_row(i, carry):
        at_x = lax.rem(gx * planes + i + nx_all - 1, nx_all)
        for row in range(rows + 2):
            at_y = lax.rem(y_tile * rows + row + ny_all - 1, ny_all)
            hb[i, LEAD - 1 + row : LEAD + row] = jnp.full((1, 128), heights[at_x, at_y], jnp.int32)
        return carry

    lax.fori_loop(0, planes + 2, height_row, 0)
    group = lane // width
    for dx in range(-1, 2):
        for band in range(2):
            packed = hb[dx + 1, 8 * band : 8 * band + 8]
            for p in range(1, planes):
                packed = jnp.where(group >= p, hb[p + dx + 1, 8 * band : 8 * band + 8], packed)
            hs[dx + 1, 8 * band : 8 * band + 8] = packed

    def own_rows(x, carry):
        for c in range(3):
            for half in range(2):
                plain[c, half, x + LEAD, LEAD : LEAD + rows] = x_disp[0, c, 2 * x + half]
        for k in range(len(BONDS)):
            for half in range(2):
                gains[k, 2 * x + half] = 10.0 / rest[k, x, 0, :, half * 128 : half * 128 + 128]
        return carry

    lax.fori_loop(0, planes, own_rows, 0)

    def count_column(i, carry):
        for j in range(ny_all):
            carry = carry + jnp.clip(heights[i, j], 0, z_tiles * cols)
        return carry

    atoms = lax.fori_loop(0, nx_all, count_column, jnp.zeros((), jnp.int32))
    receive(NEAR)
    place(NEAR, 0, 1)
    strips_of_displacement(NEAR)
    shift_main(range(3), 1, 1)
    for q in range(3):
        shift_own(q, SHIFTS_NEAR)

    def bond_sums(far, layer, height_of, length_of, gain_of, keep):
        mine = shifted_own(far)
        height = height_of(HERE)
        here = (layer >= 0) & (layer < height)
        density = jnp.zeros((8, 128), F32)
        energy = jnp.zeros((8, 128), F32)
        room = jnp.zeros((8, 128), F32)
        for k, d in enumerate(BONDS):
            s = separation(far, mine, d)
            r_sq = s[0] * s[0] + s[1] * s[1] + s[2] * s[2]
            inv_r = lax.rsqrt(r_sq)
            radius = r_sq * inv_r
            partner = (layer < height_of(d) - d[2]) & (layer >= -d[2])
            paired = partner & here
            decay = jnp.exp(3.0 - 3.0 * radius)
            cut = jnp.maximum(1.0 - r_sq * (1.0 / CUTOFF_SQ), 0.0)
            cut_value = cut * cut
            gain = gain_of(k)
            strain = (radius - length_of(k)) * gain
            squared = strain * strain
            lifted = jnp.exp(8.0 * squared)
            density = density + jnp.where(partner, decay * cut_value, 0.0)
            energy = energy + jnp.where(paired, lifted, 0.0)
            room = room + jnp.where(paired, 1.0 - squared, 0.0)
            if keep is not None:
                scale = jnp.where(paired, inv_r, 0.0)
                cut_slope = (-4.0 / CUTOFF_SQ) * radius * cut
                bonds[keep, k, 0] = scale * 0.6 * (decay * decay) * (cut_slope - 6.0 * cut_value)
                bonds[keep, k, 1] = scale * decay * (cut_slope - 3.0 * cut_value)
                strain_slope = scale * (2.0 * strain * gain)
                bonds[keep, k, 2] = strain_slope * (8.0 * lifted)
                bonds[keep, k, 3] = strain_slope
        return density, energy, room

    def main_layer(half):
        return lane + (z_tile * cols + half * 128)

    strip_layer = z_tile * cols + jnp.where(spot < 2 * ext, spot - ext, spot + (cols - width + ext))

    def main_height(x):
        return lambda d: hb[x + 1 + d[0], LEAD + d[1] : LEAD + d[1] + 8]

    def strip_height(d):
        return hs[d[0] + 1, LEAD + d[1] : LEAD + d[1] + 8]

    def embed_slope(density):
        return -0.5 * lax.rsqrt(density + 0.5)

    def bond_pass(i, x, half):
        density, energy, room = bond_sums(
            main_far(x, half),
            main_layer(half),
            main_height(x),
            lambda k: rest[k, x, 0, :, half * 128 : half * 128 + 128],
            lambda k: gains[k, i],
            i,
        )
        put(ENERGY, 0, Q_ENERGY, x, half, energy)
        put(SLOPES, 0, Q_EMBED, x, half, embed_slope(density))
        part[i, 0] = room

    tiles(bond_pass)
    for copy in copies[NEAR][-2:]:
        copy.wait_recv()
    for k in range(len(BONDS)):
        length = blend(rest_in[0, k], rest_out[k], rest_in[1, k])
        rest_strip[k] = length
        gains[k, n_tiles] = 10.0 / length
    density, energy, room = bond_sums(
        own_far(0), strip_layer, strip_height, lambda k: rest_strip[k], lambda k: gains[k, n_tiles], None
    )
    x_energy[0, 0, n_tiles] = energy
    x_slopes[0, 0, n_tiles] = embed_slope(density)
    part[n_tiles, 0] = room
    pack(ENERGY)
    send(ENERGY)

    receive(FAR)
    place(FAR, 0, 3)
    strips_of_displacement(FAR)
    shift_main(range(3), 3, 3)
    for q in range(3):
        shift_own(q, SHIFTS)

    def insides(far, i, keep):
        mine = shifted_own(far)
        for k, d in enumerate(REACH):
            s = separation(far, mine, d)
            r_sq = s[0] * s[0] + s[1] * s[1] + s[2] * s[2]
            inside = jnp.maximum(1.0 - r_sq * (1.0 / REACH_SQ), 0.0)
            squares[i, k] = inside * inside
            if keep:
                for c in range(3):
                    pulls[i, k, c] = inside * s[c]

    tiles(lambda i, x, half: insides(main_far(x, half), i, True))
    insides(own_far(0), n_tiles, False)
    receive(ENERGY)
    place(ENERGY, Q_ENERGY, 3)
    shift_main([Q_ENERGY], 3, 3)
    shift_own(Q_ENERGY, SHIFTS)
    first[...] = jnp.zeros_like(first)

    def tapered(q, far, i):
        sums_of = [jnp.zeros((8, 128), F32) for _ in range(4)]
        for k, d in enumerate(REACH):
            sums_of[k % 4] = sums_of[k % 4] + squares[i, k] * far(q, d)
        return (sums_of[0] + sums_of[1]) + (sums_of[2] + sums_of[3])

    def smooth(far, i, here):
        total = 1.0 + far(Q_ENERGY, HERE) + tapered(Q_ENERGY, far, i)
        room = part[i, 0]
        value = jnp.log(total) * 0.125
        share = 1.0 / (1.0 + value * value)
        gain = 0.08 * share
        adjoint = room * 0.08 * (-2.0 * value) * (share * share) / (8.0 * total)
        return jnp.where(here, adjoint, 0.0), gain, room

    def smooth_pass(i, x, half):
        here = main_layer(half) < main_height(x)(HERE)
        adjoint, gain, room = smooth(main_far(x, half), i, here)
        put(ADJOINT, 0, Q_ADJOINT, x, half, adjoint)
        put(SLOPES, 1, Q_GAIN, x, half, gain)
        first[...] += jnp.where(here, jnp.exp(gain * room * 2.0), 0.0)

    each_tile(smooth_pass)
    here = (strip_layer >= 0) & (strip_layer < strip_height(HERE))
    adjoint, gain, room = smooth(own_far(0), n_tiles, here)
    x_adjoint[0, 0, n_tiles] = adjoint
    x_slopes[0, 1, n_tiles] = gain
    pack(ADJOINT)
    send(ADJOINT)
    pack(SLOPES)
    send(SLOPES)
    sums[0] = jnp.sum(first[...], axis=0, keepdims=True)

    def reduction(k):
        to = lax.rem(rank + k, n_dev)
        return pltpu.make_async_remote_copy(
            src_ref=sums.at[0],
            dst_ref=sums.at[k],
            send_sem=red_send.at[k],
            recv_sem=red_recv.at[k],
            device_id=(to // n_yz, lax.rem(to, n_yz)),
            device_id_type=MESH,
        )

    def spread(k, carry):
        reduction(k).start()
        return carry

    lax.fori_loop(1, n_dev, spread, 0)

    def energy_pull(i, x, half):
        far = main_far(x, half)
        total = [jnp.zeros((8, 128), F32) for _ in range(3)]
        for k, d in enumerate(REACH):
            energy = far(Q_ENERGY, d)
            total = [total[c] + pulls[i, k, c] * energy for c in range(3)]
        for c in range(3):
            part[i, 1 + c] = total[c]

    tiles(energy_pull)

    receive(ADJOINT)
    place(ADJOINT, Q_ADJOINT, 3)
    shift_main([Q_ADJOINT], 3, 3)
    shift_own(Q_ADJOINT, SHIFTS)

    def lambda_pass(i, x, half):
        far = main_far(x, half)
        put(LAMBDA, 0, Q_LAMBDA, x, half, far(Q_ADJOINT, HERE) + tapered(Q_ADJOINT, far, i))

    each_tile(lambda_pass)
    x_lambda[0, 0, n_tiles] = own_far(0)(Q_ADJOINT, HERE) + tapered(Q_ADJOINT, own_far(0), n_tiles)
    pack(LAMBDA)
    send(LAMBDA)

    def adjoint_pull(i, x, half):
        far = main_far(x, half)
        adjoint = far(Q_ADJOINT, HERE)
        energy = far(Q_ENERGY, HERE)
        total = [jnp.zeros((8, 128), F32) for _ in range(3)]
        for k, d in enumerate(REACH):
            other = far(Q_ADJOINT, d)
            total = [total[c] + pulls[i, k, c] * other for c in range(3)]
        for c in range(3):
            part[i, 1 + c] = (-4.0 / REACH_SQ) * (adjoint * part[i, 1 + c] + energy * total[c])

    tiles(adjoint_pull)
    receive(SLOPES)
    place(SLOPES, Q_EMBED, 1)
    shift_main([Q_EMBED, Q_GAIN], 1, 1)

    def collect(k, carry):
        reduction(k).wait_recv()
        return carry

    lax.fori_loop(1, n_dev, collect, 0)
    total = jnp.sum(jnp.sum(sums[...], axis=0), axis=1, keepdims=True)
    boost[...] = jnp.broadcast_to(total, (1, 128)) / jnp.full((1, 128), atoms.astype(F32))

    def finish(k, carry):
        reduction(k).wait_send()
        return carry

    lax.fori_loop(1, n_dev, finish, 0)
    for r in range(LAMBDA):
        for copy in copies[r]:
            copy.wait_send()
    receive(LAMBDA)
    place(LAMBDA, Q_LAMBDA, 1)
    shift_main([Q_LAMBDA], 1, 1)

    def final_pass(i, x, half):
        far = main_far(x, half)
        mine = shifted_own(far)
        lam, embed, gain = far(Q_LAMBDA, HERE), far(Q_EMBED, HERE), far(Q_GAIN, HERE)
        force = [part[i, 1 + c] for c in range(3)]
        for k, d in enumerate(BONDS):
            s = separation(far, mine, d)
            weight = (
                bonds[i, k, 0]
                + (embed + far(Q_EMBED, d)) * bonds[i, k, 1]
                + (lam + far(Q_LAMBDA, d)) * bonds[i, k, 2]
                - (gain + far(Q_GAIN, d)) * bonds[i, k, 3]
            )
            force = [force[c] + weight * s[c] for c in range(3)]
        span = slice(half * 128, half * 128 + 128)
        for c in range(3):
            forces[c, x, 0, :, span] = force[c]

    each_tile(final_pass)
    for copy in copies[LAMBDA]:
        copy.wait_send()


def body(n_gx, n_yz, displacement, velocity, rest_length, heights):
    _, planes, _, rows, cols = displacement.shape
    z_tiles = n_yz // (heights.shape[1] // rows)
    slots = 2 if n_gx == 2 else 3
    n_dev = n_gx * n_yz
    n_tiles = 2 * planes
    n_bonds = len(BONDS)
    n_msg = 3 + 2 * slots + 6 * slots + 2
    y_rows = [count * (n_tiles + 1) * (high - low + 1) for count, low, high in ROUNDS]
    scratch = [pltpu.VMEM((slots, count, n_tiles + 1, 8, 128), F32) for count in (3, 1, 1, 2, 1)]
    scratch += [pltpu.VMEM((2, n, 128), F32) for n in y_rows]
    scratch += [pltpu.VMEM((2, slots, n, 128), F32) for n in y_rows]
    scratch += [
        pltpu.VMEM((2, slots, 3, 8, 128), F32),
        pltpu.VMEM((2, 3, LEAD, 128), F32),
        pltpu.VMEM((2, 2, slots, 3, LEAD, 128), F32),
        pltpu.VMEM((n_bonds, 8, 128), F32),
        pltpu.VMEM((2, n_bonds, 8, 128), F32),
        pltpu.VMEM((8, 2, planes + 2 * LEAD, BAND, 128), F32),
        pltpu.VMEM((8, 2, planes + 2 * LEAD, BAND, 128), F32),
        pltpu.VMEM((8, 7, 2, planes + 2 * LEAD, BAND, 128), F32),
        pltpu.VMEM((8, slots, BAND, 128), F32),
        pltpu.VMEM((5, 7, 7, BAND, 128), F32),
        pltpu.VMEM((planes + 2, BAND, 128), jnp.int32),
        pltpu.VMEM((3, BAND, 128), jnp.int32),
        pltpu.VMEM((n_tiles + 1, len(REACH), 8, 128), F32),
        pltpu.VMEM((n_tiles, len(REACH), 3, 8, 128), F32),
        pltpu.VMEM((n_tiles, n_bonds, 4, 8, 128), F32),
        pltpu.VMEM((n_tiles + 1, 4, 8, 128), F32),
        pltpu.VMEM((8, 128), F32),
        pltpu.VMEM((n_dev, 1, 128), F32),
        pltpu.VMEM((n_bonds, n_tiles + 1, 8, 128), F32),
        pltpu.VMEM((n_bonds, 8, 128), F32),
        pltpu.VMEM(rest_length.shape, F32),
        pltpu.SMEM(heights.shape, jnp.int32),
        pltpu.SemaphoreType.DMA((len(ROUNDS), n_msg)),
        pltpu.SemaphoreType.DMA((len(ROUNDS), n_msg)),
        pltpu.SemaphoreType.DMA((n_dev,)),
        pltpu.SemaphoreType.DMA((n_dev,)),
        pltpu.SemaphoreType.DMA((2 + n_tiles,)),
    ]
    vmem = pl.BlockSpec(memory_space=pltpu.VMEM)
    hbm = pl.BlockSpec(memory_space=pltpu.HBM)
    forces, boost = pl.pallas_call(
        functools.partial(kernel, n_gx, n_yz, z_tiles),
        out_shape=(
            pltpu.VMEM(displacement.shape, F32),
            pltpu.VMEM((1, 128), F32),
        ),
        in_specs=[hbm, hbm, hbm],
        out_specs=(vmem, vmem),
        scratch_shapes=scratch,
        compiler_params=pltpu.CompilerParams(
            collective_id=0, has_side_effects=True, vmem_limit_bytes=64_000_000
        ),
    )(heights, displacement, rest_length)
    new_vel = velocity + 0.2 * forces
    return displacement + 0.05 * new_vel, new_vel, boost[0, 0]


def solution(mesh):
    tiled = P(None, "gx", "yz", None, None)
    sizes = (mesh.shape["gx"], mesh.shape["yz"])
    return jax.shard_map(
        functools.partial(body, *sizes),
        mesh=mesh,
        in_specs=(tiled, tiled, tiled, P()),
        out_specs=(tiled, tiled, P()),
        check_vma=False,
    )
```

```python
import functools

import jax
import jax.numpy as jnp
from jax import lax
from jax.experimental import pallas as pl
from jax.experimental.pallas import tpu as pltpu
from jax.sharding import PartitionSpec as P

CUTOFF_SQ = 1.5 * 1.5
REACH_SQ = 3.5 * 3.5
F32 = jnp.float32
MESH = pl.DeviceIdType.MESH


def list_offsets(reach_sq, forward_only):
    chosen = []
    for ax in range(-3, 4):
        for ay in range(-3, 4):
            for az in range(-3, 4):
                length_sq = ax * ax + ay * ay + az * az
                if 0 < length_sq <= reach_sq:
                    if not forward_only or (ax, ay, az) > (0, 0, 0):
                        chosen.append((ax, ay, az))
    return chosen


FORWARD = list_offsets(2, True)
BONDS = FORWARD + [(-v[0], -v[1], -v[2]) for v in FORWARD]
REACH = list_offsets(9, False)
SHIFTS = [(dx, dz) for dx in range(-3, 4) for dz in range(-3, 4) if dx * dx + dz * dz <= 9]
SHIFTS_NEAR = [(dx, dz) for dx in range(-1, 2) for dz in range(-1, 2)]

NEAR, FAR, ENERGY, ADJOINT, SLOPES, LAMBDA = range(6)
ROUNDS = [(3, 1, 1), (3, 2, 3), (1, 1, 3), (1, 1, 3), (2, 1, 1), (1, 1, 1)]
Q_ENERGY, Q_ADJOINT, Q_LAMBDA, Q_EMBED, Q_GAIN = range(3, 8)
LEAD = 4
BAND = 16


def kernel(n_gx, n_yz, z_tiles, heights_hbm, disp, rest_hbm, forces, boost, *scratch):
    (x_disp, x_energy, x_adjoint, x_slopes, x_lambda) = scratch[0:5]
    ys = scratch[5:11]
    yr = scratch[11:17]
    scratch = scratch[3:]
    (z_mid, z_edge_out, z_edge, rest_out, rest_in) = scratch[14:19]
    (plain, edges, store, strip, strip_own, hb, hs, squares, pulls, bonds, part, first, sums) = scratch[19:32]
    (gains, rest_strip, rest, heights) = scratch[32:36]
    (send_sem, recv_sem, red_send, red_recv, load_sem) = scratch[36:41]
    x_of = [x_disp, x_disp, x_energy, x_adjoint, x_slopes, x_lambda]
    nx_all, ny_all = heights.shape
    loads = [
        pltpu.make_async_copy(heights_hbm, heights, load_sem.at[0]),
        pltpu.make_async_copy(rest_hbm, rest, load_sem.at[1]),
    ]
    planes, rows, cols = disp.shape[1], disp.shape[3], disp.shape[4]
    for half in range(2):
        for p in range(planes):
            loads.append(
                pltpu.make_async_copy(
                    disp.at[:, p, 0, :, half * 128 : half * 128 + 128],
                    x_disp.at[0, :, 2 * p + half],
                    load_sem.at[2 + 2 * p + half],
                )
            )
    for load in loads[2:] + loads[:2]:
        load.start()
    n_tiles = 2 * planes
    width = 128 // planes
    ext = width // 4
    y_tiles = n_yz // z_tiles
    gx = lax.axis_index("gx")
    me = lax.axis_index("yz")
    h = me + z_tiles // 2
    y_tile = lax.rem(h // z_tiles, y_tiles)
    z_tile = lax.rem(h, z_tiles)
    x_steps = [0, 1] if n_gx == 2 else [0, 1, -1]
    n_slots = len(x_steps)
    steps = [0, 1, -1]
    left_slot, right_slot = 1, n_slots - 1

    targets = {}

    def target(a, b, c):
        if (a, b, c) not in targets:
            to_y = lax.rem(y_tile + b + y_tiles, y_tiles)
            to_z = lax.rem(z_tile + c + z_tiles, z_tiles)
            to = lax.rem(to_y * z_tiles + to_z + n_yz - z_tiles // 2, n_yz)
            targets[(a, b, c)] = (lax.rem(gx + a + n_gx, n_gx), to)
        return targets[(a, b, c)]

    n_dev = n_gx * n_yz
    rank = gx * n_yz + me
    barrier = pltpu.get_barrier_semaphore()

    def greet(k, carry):
        to = lax.rem(rank + k, n_dev)
        pl.semaphore_signal(barrier, inc=1, device_id=(to // n_yz, lax.rem(to, n_yz)), device_id_type=MESH)
        return carry

    lax.fori_loop(1, n_dev, greet, 0)

    lane = lax.broadcasted_iota(jnp.int32, (8, 128), 1)
    spot = lax.rem(lane, width)

    def x_messages(r):
        buf = x_of[r]
        top = n_tiles - 2
        if r in (NEAR, SLOPES, LAMBDA):
            out = [
                (buf.at[0, :, top : n_tiles + 1], buf.at[left_slot, :, top : n_tiles + 1], 1),
                (buf.at[0, :, 0:2], buf.at[right_slot, :, 0:2], -1),
            ]
            if n_slots == 3:
                out.append((buf.at[0, :, n_tiles], buf.at[right_slot, :, n_tiles], -1))
        elif r == FAR:
            if n_slots == 2:
                out = [(buf.at[0, :, 2:top], buf.at[1, :, 2:top], 1)]
            else:
                out = [
                    (buf.at[0, :, 0:top], buf.at[left_slot, :, 0:top], 1),
                    (buf.at[0, :, 2:n_tiles], buf.at[right_slot, :, 2:n_tiles], -1),
                ]
        else:
            out = [(buf.at[0], buf.at[ai], x_steps[ai]) for ai in range(1, n_slots)]
        return [(src, dst, a, 0, 0) for src, dst, a in out]

    def messages(r):
        out = []
        if r == NEAR:
            for ai, a in reversed(list(enumerate(x_steps))):
                for ci in range(2):
                    for bi in range(2):
                        out.append((z_edge_out.at[bi], z_edge.at[ci, bi, ai], a, steps[1 + bi], steps[1 + ci]))
                    out.append((x_disp.at[0, :, n_tiles], z_mid.at[ci, ai], a, 0, steps[1 + ci]))
        far = []
        for ai, a in reversed(list(enumerate(x_steps))):
            for bi in range(2):
                far.append((ys[r].at[bi], yr[r].at[bi, ai], a, steps[1 + bi], 0))
        out = sorted(far + out, key=lambda m: -sum(abs(v) for v in m[2:]))
        out = out + x_messages(r)
        if r == NEAR:
            for ci in range(2):
                out.append((rest_out, rest_in.at[ci], 0, 0, steps[1 + ci]))
        return [
            pltpu.make_async_remote_copy(
                src_ref=src,
                dst_ref=dst,
                send_sem=send_sem.at[r, i],
                recv_sem=recv_sem.at[r, i],
                device_id=target(a, b, c),
                device_id_type=MESH,
            )
            for i, (src, dst, a, b, c) in enumerate(out)
        ]

    copies = [messages(r) for r in range(len(ROUNDS))]

    def pack(r):
        count, low, high = ROUNDS[r]
        n_rows = high - low + 1
        for q in range(count):
            for t in range(n_tiles + 1):
                at = (q * (n_tiles + 1) + t) * n_rows
                ys[r][0, at : at + n_rows] = x_of[r][0, q, t, rows - high : rows - low + 1]
                ys[r][1, at : at + n_rows] = x_of[r][0, q, t, low - 1 : high]

    def send(r):
        for copy in copies[r][: len(copies[r]) - (2 if r == NEAR else 0)]:
            copy.start()

    def receive(r):
        for copy in copies[r][: len(copies[r]) - (2 if r == NEAR else 0)]:
            copy.wait_recv()

    def place_of(xp):
        if xp < 0:
            return left_slot, xp + planes
        if xp < planes:
            return 0, xp
        return right_slot, xp - planes

    def ghosts(r, q, t, slot):
        count, low, high = ROUNDS[r]
        n_rows = high - low + 1
        at = (q * (n_tiles + 1) + t) * n_rows
        return [
            (LEAD - high, LEAD - low + 1, yr[r][0, slot, at : at + n_rows]),
            (LEAD + rows + low - 1, LEAD + rows + high, yr[r][1, slot, at : at + n_rows]),
        ]

    def place(r, base, reach):
        for q in range(ROUNDS[r][0]):
            for xp in range(-reach, planes + reach):
                slot, plane = place_of(xp)
                at = xp + LEAD
                for half in range(2):
                    t = 2 * plane + half
                    if slot:
                        plain[base + q, half, at, LEAD : LEAD + rows] = x_of[r][slot, q, t]
                    for lo, hi, value in ghosts(r, q, t, slot) + (ghosts(NEAR, q, t, slot) if r == FAR else []):
                        plain[base + q, half, at, lo:hi] = value
            for slot in range(n_slots):
                if r != NEAR and r != FAR:
                    strip[base + q, slot, LEAD : LEAD + rows] = x_of[r][slot, q, n_tiles]
                    for lo, hi, value in ghosts(r, q, n_tiles, slot):
                        strip[base + q, slot, lo:hi] = value

    def blend(below, own, above):
        return jnp.where(spot < ext, below, jnp.where(spot >= width - ext, above, own))

    def strips_of_displacement(r):
        lane4 = lane[0:4]
        for q in range(3):
            for slot in range(n_slots):
                if r == NEAR:
                    strip[q, slot, LEAD : LEAD + rows] = blend(z_mid[0, slot, q], x_disp[slot, q, n_tiles], z_mid[1, slot, q])
                for bi, (lo, hi, value) in enumerate(ghosts(r, q, n_tiles, slot)):
                    first_row = lo - (0 if bi == 0 else LEAD + rows)
                    span = slice(first_row, first_row + hi - lo)
                    n = hi - lo
                    spot_n = spot[0:n]
                    strip[q, slot, lo:hi] = jnp.where(
                        spot_n < ext,
                        z_edge[0, bi, slot, q, span],
                        jnp.where(spot_n >= width - ext, z_edge[1, bi, slot, q, span], value),
                    )

    def shift_main(fields, reach, depth):
        inner = min(reach, max(1, reach - 1))
        spans = []
        for q in fields:
            for xp in range(-inner, planes + inner):
                for band in range(2):
                    spans.append((q, xp, band, slice(8 * band, 8 * band + 8)))
        for q, xp, band, span in spans:
            slot, plane = place_of(xp)
            edge = strip[q, slot, span]
            edges[q, 0, xp + LEAD, span] = pltpu.roll(edge, (128 - ext - width * plane) % 128, 1)
            edges[q, 1, xp + LEAD, span] = pltpu.roll(edge, (ext - width * plane - width) % 128, 1)
        for q, xp, band, span in spans:
            at = xp + LEAD
            t1 = plain[q, 0, at, span]
            t2 = plain[q, 1, at, span]
            low = edges[q, 0, at, span]
            high = edges[q, 1, at, span]
            for dz in range(1, depth + 1):
                if dz == 3 and not 3 - reach <= xp < planes + reach - 3:
                    continue
                up = lane < dz
                down = lane >= 128 - dz
                store[q, 3 + dz, 0, at, span] = pltpu.roll(jnp.where(up, t2, t1), 128 - dz, 1)
                store[q, 3 + dz, 1, at, span] = pltpu.roll(jnp.where(up, high, t2), 128 - dz, 1)
                store[q, 3 - dz, 0, at, span] = pltpu.roll(jnp.where(down, low, t1), dz, 1)
                store[q, 3 - dz, 1, at, span] = pltpu.roll(jnp.where(down, t1, t2), dz, 1)

    def shift_own(q, shifts):
        for band in range(2):
            span = slice(8 * band, 8 * band + 8)
            own, left, right = strip[q, 0, span], strip[q, left_slot, span], strip[q, right_slot, span]
            for dx, dz in shifts:
                s = width * dx + dz
                if s > 0:
                    value = pltpu.roll(jnp.where(lane >= s, own, right), 128 - s, 1)
                elif s < 0:
                    value = pltpu.roll(jnp.where(lane < 128 + s, own, left), -s, 1)
                else:
                    value = own
                strip_own[q, dx + 3, dz + 3, span] = value

    def cell(q, dz, half):
        return store.at[q, dz + 3, half] if dz else plain.at[q, half]

    def main_far(x, half):
        def far(q, d):
            return cell(q, d[2], half)[x + LEAD + d[0], LEAD + d[1] : LEAD + d[1] + 8]

        return far

    def own_far(row):
        def far(q, d):
            at = LEAD + row + d[1]
            return strip_own[q, d[0] + 3, d[2] + 3, at : at + 8]

        return far

    HERE = (0, 0, 0)

    def shifted_own(far):
        mine = [far(c, HERE) for c in range(3)]
        return [{v: (mine[c] - float(v) if v else mine[c]) for v in range(-3, 4)} for c in range(3)]

    def separation(far, mine, d):
        return [far(c, d) - mine[c][d[c]] for c in range(3)]

    def tiles(body):
        def step(x, carry):
            for half in range(2):
                body(2 * x + half, x, half)
            return carry

        lax.fori_loop(0, planes, step, 0)

    def each_tile(body):
        for i in range(n_tiles):
            body(i, i // 2, i % 2)

    def put(r, q, field, x, half, value):
        x_of[r][0, q, 2 * x + half] = value
        plain[field, half, x + LEAD, LEAD : LEAD + rows] = value

    def window(tile_of):
        packed = jnp.zeros((8, 128), F32)
        for p in range(planes):
            both = jnp.where(lane < 64, tile_of(p, 0), tile_of(p, 1))
            moved = pltpu.roll(both, (ext + width * p) % 128, 1)
            packed = moved if p == 0 else jnp.where(lane >= width * p, moved, packed)
        return jnp.where(spot < 2 * ext, packed, pltpu.roll(packed, 2 * ext, 1))

    for load in loads[2:]:
        load.wait()
    for c in range(3):
        x_disp[0, c, n_tiles] = window(lambda p, half: x_disp[0, c, 2 * p + half])
        for bi in range(2):
            z_edge_out[bi, c] = x_disp[0, c, n_tiles, (rows - LEAD) * (1 - bi) : (rows - LEAD) * (1 - bi) + LEAD]
    pack(NEAR)
    pl.semaphore_wait(barrier, n_dev - 1)
    send(NEAR)
    loads[1].wait()
    for k in range(len(BONDS)):
        rest_out[k] = window(lambda p, half: rest[k, p, 0, :, half * 128 : half * 128 + 128])
    for copy in copies[NEAR][-2:]:
        copy.start()
    pack(FAR)
    send(FAR)

    loads[0].wait()

    def height_row(i, carry):
        at_x = lax.rem(gx * planes + i + nx_all - 1, nx_all)
        for row in range(rows + 2):
            at_y = lax.rem(y_tile * rows + row + ny_all - 1, ny_all)
            hb[i, LEAD - 1 + row : LEAD + row] = jnp.full((1, 128), heights[at_x, at_y], jnp.int32)
        return carry

    lax.fori_loop(0, planes + 2, height_row, 0)
    group = lane // width
    for dx in range(-1, 2):
        for band in range(2):
            packed = hb[dx + 1, 8 * band : 8 * band + 8]
            for p in range(1, planes):
                packed = jnp.where(group >= p, hb[p + dx + 1, 8 * band : 8 * band + 8], packed)
            hs[dx + 1, 8 * band : 8 * band + 8] = packed

    def own_rows(x, carry):
        for c in range(3):
            for half in range(2):
                plain[c, half, x + LEAD, LEAD : LEAD + rows] = x_disp[0, c, 2 * x + half]
        for k in range(len(BONDS)):
            for half in range(2):
                gains[k, 2 * x + half] = 10.0 / rest[k, x, 0, :, half * 128 : half * 128 + 128]
        return carry

    lax.fori_loop(0, planes, own_rows, 0)

    def count_column(i, carry):
        for j in range(ny_all):
            carry = carry + jnp.clip(heights[i, j], 0, z_tiles * cols)
        return carry

    atoms = lax.fori_loop(0, nx_all, count_column, jnp.zeros((), jnp.int32))
    receive(NEAR)
    place(NEAR, 0, 1)
    strips_of_displacement(NEAR)
    shift_main(range(3), 1, 1)
    for q in range(3):
        shift_own(q, SHIFTS_NEAR)

    def bond_sums(far, layer, height_of, length_of, gain_of, keep):
        mine = shifted_own(far)
        height = height_of(HERE)
        here = (layer >= 0) & (layer < height)
        density = jnp.zeros((8, 128), F32)
        energy = jnp.zeros((8, 128), F32)
        room = jnp.zeros((8, 128), F32)
        for k, d in enumerate(BONDS):
            s = separation(far, mine, d)
            r_sq = s[0] * s[0] + s[1] * s[1] + s[2] * s[2]
            inv_r = lax.rsqrt(r_sq)
            radius = r_sq * inv_r
            partner = (layer < height_of(d) - d[2]) & (layer >= -d[2])
            paired = partner & here
            decay = jnp.exp(3.0 - 3.0 * radius)
            cut = jnp.maximum(1.0 - r_sq * (1.0 / CUTOFF_SQ), 0.0)
            cut_value = cut * cut
            gain = gain_of(k)
            strain = (radius - length_of(k)) * gain
            squared = strain * strain
            lifted = jnp.exp(8.0 * squared)
            density = density + jnp.where(partner, decay * cut_value, 0.0)
            energy = energy + jnp.where(paired, lifted, 0.0)
            room = room + jnp.where(paired, 1.0 - squared, 0.0)
            if keep is not None:
                scale = jnp.where(paired, inv_r, 0.0)
                cut_slope = (-4.0 / CUTOFF_SQ) * radius * cut
                bonds[keep, k, 0] = scale * 0.6 * (decay * decay) * (cut_slope - 6.0 * cut_value)
                bonds[keep, k, 1] = scale * decay * (cut_slope - 3.0 * cut_value)
                strain_slope = scale * (2.0 * strain * gain)
                bonds[keep, k, 2] = strain_slope * (8.0 * lifted)
                bonds[keep, k, 3] = strain_slope
        return density, energy, room

    def main_layer(half):
        return lane + (z_tile * cols + half * 128)

    strip_layer = z_tile * cols + jnp.where(spot < 2 * ext, spot - ext, spot + (cols - width + ext))

    def main_height(x):
        return lambda d: hb[x + 1 + d[0], LEAD + d[1] : LEAD + d[1] + 8]

    def strip_height(d):
        return hs[d[0] + 1, LEAD + d[1] : LEAD + d[1] + 8]

    def embed_slope(density):
        return -0.5 * lax.rsqrt(density + 0.5)

    def main_bonds(i, x, half, keep):
        return bond_sums(
            main_far(x, half),
            main_layer(half),
            main_height(x),
            lambda k: rest[k, x, 0, :, half * 128 : half * 128 + 128],
            lambda k: gains[k, i],
            keep,
        )

    def bond_pass(i, x, half):
        density, energy, room = main_bonds(i, x, half, None)
        put(ENERGY, 0, Q_ENERGY, x, half, energy)
        put(SLOPES, 0, Q_EMBED, x, half, embed_slope(density))
        part[i, 0] = room

    tiles(bond_pass)
    for copy in copies[NEAR][-2:]:
        copy.wait_recv()
    for k in range(len(BONDS)):
        length = blend(rest_in[0, k], rest_out[k], rest_in[1, k])
        rest_strip[k] = length
        gains[k, n_tiles] = 10.0 / length
    density, energy, room = bond_sums(
        own_far(0), strip_layer, strip_height, lambda k: rest_strip[k], lambda k: gains[k, n_tiles], None
    )
    x_energy[0, 0, n_tiles] = energy
    x_slopes[0, 0, n_tiles] = embed_slope(density)
    part[n_tiles, 0] = room
    pack(ENERGY)
    send(ENERGY)

    receive(FAR)
    place(FAR, 0, 3)
    strips_of_displacement(FAR)
    shift_main(range(3), 3, 3)
    for q in range(3):
        shift_own(q, SHIFTS)

    def insides(far, i, keep):
        mine = shifted_own(far)
        for k, d in enumerate(REACH):
            s = separation(far, mine, d)
            r_sq = s[0] * s[0] + s[1] * s[1] + s[2] * s[2]
            inside = jnp.maximum(1.0 - r_sq * (1.0 / REACH_SQ), 0.0)
            squares[i, k] = inside * inside
            if keep:
                for c in range(3):
                    pulls[i, k, c] = inside * s[c]

    tiles(lambda i, x, half: insides(main_far(x, half), i, True))
    insides(own_far(0), n_tiles, False)
    receive(ENERGY)
    place(ENERGY, Q_ENERGY, 3)
    shift_main([Q_ENERGY], 3, 3)
    shift_own(Q_ENERGY, SHIFTS)
    first[...] = jnp.zeros_like(first)

    def tapered(q, far, i):
        sums_of = [jnp.zeros((8, 128), F32) for _ in range(4)]
        for k, d in enumerate(REACH):
            sums_of[k % 4] = sums_of[k % 4] + squares[i, k] * far(q, d)
        return (sums_of[0] + sums_of[1]) + (sums_of[2] + sums_of[3])

    def smooth(far, i, here):
        total = 1.0 + far(Q_ENERGY, HERE) + tapered(Q_ENERGY, far, i)
        room = part[i, 0]
        value = jnp.log(total) * 0.125
        share = 1.0 / (1.0 + value * value)
        gain = 0.08 * share
        adjoint = room * 0.08 * (-2.0 * value) * (share * share) / (8.0 * total)
        return jnp.where(here, adjoint, 0.0), gain, room

    def smooth_pass(i, x, half):
        here = main_layer(half) < main_height(x)(HERE)
        adjoint, gain, room = smooth(main_far(x, half), i, here)
        put(ADJOINT, 0, Q_ADJOINT, x, half, adjoint)
        put(SLOPES, 1, Q_GAIN, x, half, gain)
        first[...] += jnp.where(here, jnp.exp(gain * room * 2.0), 0.0)

    each_tile(smooth_pass)
    here = (strip_layer >= 0) & (strip_layer < strip_height(HERE))
    adjoint, gain, room = smooth(own_far(0), n_tiles, here)
    x_adjoint[0, 0, n_tiles] = adjoint
    x_slopes[0, 1, n_tiles] = gain
    pack(ADJOINT)
    send(ADJOINT)
    pack(SLOPES)
    send(SLOPES)
    sums[0] = jnp.sum(first[...], axis=0, keepdims=True)

    def reduction(k):
        to = lax.rem(rank + k, n_dev)
        return pltpu.make_async_remote_copy(
            src_ref=sums.at[0],
            dst_ref=sums.at[k],
            send_sem=red_send.at[0],
            recv_sem=red_recv.at[0],
            device_id=(to // n_yz, lax.rem(to, n_yz)),
            device_id_type=MESH,
        )

    def spread(k, carry):
        reduction(k).start()
        return carry

    lax.fori_loop(1, n_dev, spread, 0)

    def energy_pull(i, x, half):
        far = main_far(x, half)
        total = [jnp.zeros((8, 128), F32) for _ in range(3)]
        for k, d in enumerate(REACH):
            energy = far(Q_ENERGY, d)
            total = [total[c] + pulls[i, k, c] * energy for c in range(3)]
        for c in range(3):
            part[i, 1 + c] = total[c]

    tiles(energy_pull)
    for r in (NEAR, FAR, ENERGY):
        for copy in copies[r]:
            copy.wait_send()

    receive(ADJOINT)
    place(ADJOINT, Q_ADJOINT, 3)
    shift_main([Q_ADJOINT], 3, 3)
    shift_own(Q_ADJOINT, SHIFTS)

    def lambda_pass(i, x, half):
        far = main_far(x, half)
        put(LAMBDA, 0, Q_LAMBDA, x, half, far(Q_ADJOINT, HERE) + tapered(Q_ADJOINT, far, i))

    each_tile(lambda_pass)
    x_lambda[0, 0, n_tiles] = own_far(0)(Q_ADJOINT, HERE) + tapered(Q_ADJOINT, own_far(0), n_tiles)
    pack(LAMBDA)
    send(LAMBDA)
    tiles(lambda i, x, half: main_bonds(i, x, half, i))

    def adjoint_pull(i, x, half):
        far = main_far(x, half)
        adjoint = far(Q_ADJOINT, HERE)
        energy = far(Q_ENERGY, HERE)
        total = [jnp.zeros((8, 128), F32) for _ in range(3)]
        for k, d in enumerate(REACH):
            other = far(Q_ADJOINT, d)
            total = [total[c] + pulls[i, k, c] * other for c in range(3)]
        for c in range(3):
            part[i, 1 + c] = (-4.0 / REACH_SQ) * (adjoint * part[i, 1 + c] + energy * total[c])

    tiles(adjoint_pull)
    receive(SLOPES)
    place(SLOPES, Q_EMBED, 1)
    shift_main([Q_EMBED, Q_GAIN], 1, 1)

    every_sum = pltpu.make_async_remote_copy(
        src_ref=sums.at[1:n_dev],
        dst_ref=sums.at[1:n_dev],
        send_sem=red_send.at[0],
        recv_sem=red_recv.at[0],
        device_id=target(1, 0, 0),
        device_id_type=MESH,
    )
    every_sum.wait_recv()
    total = jnp.sum(jnp.sum(sums[...], axis=0), axis=1, keepdims=True)
    boost[...] = jnp.broadcast_to(total, (1, 128)) / jnp.full((1, 128), atoms.astype(F32))

    every_sum.wait_send()
    for r in (ADJOINT, SLOPES):
        for copy in copies[r]:
            copy.wait_send()
    receive(LAMBDA)
    place(LAMBDA, Q_LAMBDA, 1)
    shift_main([Q_LAMBDA], 1, 1)

    def final_pass(i, x, half):
        far = main_far(x, half)
        mine = shifted_own(far)
        lam, embed, gain = far(Q_LAMBDA, HERE), far(Q_EMBED, HERE), far(Q_GAIN, HERE)
        force = [part[i, 1 + c] for c in range(3)]
        for k, d in enumerate(BONDS):
            s = separation(far, mine, d)
            weight = (
                bonds[i, k, 0]
                + (embed + far(Q_EMBED, d)) * bonds[i, k, 1]
                + (lam + far(Q_LAMBDA, d)) * bonds[i, k, 2]
                - (gain + far(Q_GAIN, d)) * bonds[i, k, 3]
            )
            force = [force[c] + weight * s[c] for c in range(3)]
        span = slice(half * 128, half * 128 + 128)
        for c in range(3):
            forces[c, x, 0, :, span] = force[c]

    each_tile(final_pass)
    for copy in copies[LAMBDA]:
        copy.wait_send()


def body(n_gx, n_yz, displacement, velocity, rest_length, heights):
    _, planes, _, rows, cols = displacement.shape
    z_tiles = n_yz // (heights.shape[1] // rows)
    slots = 2 if n_gx == 2 else 3
    n_dev = n_gx * n_yz
    n_tiles = 2 * planes
    n_bonds = len(BONDS)
    n_msg = 3 + 2 * slots + 6 * slots + 2
    y_rows = [count * (n_tiles + 1) * (high - low + 1) for count, low, high in ROUNDS]
    scratch = [pltpu.VMEM((slots, count, n_tiles + 1, 8, 128), F32) for count in (3, 1, 1, 2, 1)]
    scratch += [pltpu.VMEM((2, n, 128), F32) for n in y_rows]
    scratch += [pltpu.VMEM((2, slots, n, 128), F32) for n in y_rows]
    scratch += [
        pltpu.VMEM((2, slots, 3, 8, 128), F32),
        pltpu.VMEM((2, 3, LEAD, 128), F32),
        pltpu.VMEM((2, 2, slots, 3, LEAD, 128), F32),
        pltpu.VMEM((n_bonds, 8, 128), F32),
        pltpu.VMEM((2, n_bonds, 8, 128), F32),
        pltpu.VMEM((8, 2, planes + 2 * LEAD, BAND, 128), F32),
        pltpu.VMEM((8, 2, planes + 2 * LEAD, BAND, 128), F32),
        pltpu.VMEM((8, 7, 2, planes + 2 * LEAD, BAND, 128), F32),
        pltpu.VMEM((8, slots, BAND, 128), F32),
        pltpu.VMEM((5, 7, 7, BAND, 128), F32),
        pltpu.VMEM((planes + 2, BAND, 128), jnp.int32),
        pltpu.VMEM((3, BAND, 128), jnp.int32),
        pltpu.VMEM((n_tiles + 1, len(REACH), 8, 128), F32),
        pltpu.VMEM((n_tiles, len(REACH), 3, 8, 128), F32),
        pltpu.VMEM((n_tiles, n_bonds, 4, 8, 128), F32),
        pltpu.VMEM((n_tiles + 1, 4, 8, 128), F32),
        pltpu.VMEM((8, 128), F32),
        pltpu.VMEM((n_dev, 1, 128), F32),
        pltpu.VMEM((n_bonds, n_tiles + 1, 8, 128), F32),
        pltpu.VMEM((n_bonds, 8, 128), F32),
        pltpu.VMEM(rest_length.shape, F32),
        pltpu.SMEM(heights.shape, jnp.int32),
        pltpu.SemaphoreType.DMA((len(ROUNDS), n_msg)),
        pltpu.SemaphoreType.DMA((len(ROUNDS), n_msg)),
        pltpu.SemaphoreType.DMA((n_dev,)),
        pltpu.SemaphoreType.DMA((n_dev,)),
        pltpu.SemaphoreType.DMA((2 + n_tiles,)),
    ]
    vmem = pl.BlockSpec(memory_space=pltpu.VMEM)
    hbm = pl.BlockSpec(memory_space=pltpu.HBM)
    forces, boost = pl.pallas_call(
        functools.partial(kernel, n_gx, n_yz, z_tiles),
        out_shape=(
            pltpu.VMEM(displacement.shape, F32),
            pltpu.VMEM((1, 128), F32),
        ),
        in_specs=[hbm, hbm, hbm],
        out_specs=(vmem, vmem),
        scratch_shapes=scratch,
        compiler_params=pltpu.CompilerParams(
            collective_id=0, has_side_effects=True, vmem_limit_bytes=64_000_000
        ),
    )(heights, displacement, rest_length)
    new_vel = velocity + 0.2 * forces
    return displacement + 0.05 * new_vel, new_vel, boost[0, 0]


def solution(mesh):
    tiled = P(None, "gx", "yz", None, None)
    sizes = (mesh.shape["gx"], mesh.shape["yz"])
    return jax.shard_map(
        functools.partial(body, *sizes),
        mesh=mesh,
        in_specs=(tiled, tiled, tiled, P()),
        out_specs=(tiled, tiled, P()),
        check_vma=False,
    )
```
